32 devices in a mesh: groups: 2 (over y), row: 4 (over z), col: 4 (over x, core).
Axes of the slice: x: 2, y: 2, z: 4, core: 2. Of those that a mesh axis runs over, the one named last changes fastest.
Arguments:
- queries: bfloat16 [4096, 1024], P(('groups', 'row'), 'col'), parts along dimension 0, may hold values from -64 to 64
- keys: bfloat16 [4096, 1024], P(('groups', 'col'), 'row'), parts along dimension 0, may hold values from -6 to 6
- values: bfloat16 [4096, 1024], P(('groups', 'col'), 'row'), parts along dimension 0, may hold values from -6 to 6
- cotangent: bfloat16 [4096, 1024], P(('groups', 'row'), 'col'), parts along dimension 0, may hold values from -6 to 6
- block_lists: int32 [32, 16], P(('groups', 'row')), parts along dimension 0, may hold values from 0 to 15, as said below
- block_counts: int32 [32], P(('groups', 'row')), parts along dimension 0, may hold values from 1 to 16, as said below
Outputs:
- attended: bfloat16 [4096, 1024], P(('groups', 'row'), 'col'), parts along dimension 0
- grad_queries: bfloat16 [4096, 1024], P(('groups', 'row'), 'col'), parts along dimension 0
- grad_keys: bfloat16 [4096, 1024], P(('groups', 'col'), 'row'), parts along dimension 0
- grad_values: bfloat16 [4096, 1024], P(('groups', 'col'), 'row'), parts along dimension 0
The draws below stay inside these ranges and needn't reach their ends.
There are 2 independent parts, one for each index of `groups`. The reference program is written for one: setup_inputs(seed, part) draws one part's arguments, and reference() takes and returns one part's arrays. A program takes and returns all parts, laid end to end along the dimension named above; each array names one. Nothing has to cross between parts.
Inputs may be any that keep to these rules, and one draw needn't show every extreme that they name: `block_lists`: each row lists 16 distinct blocks; its first entry is the query block itself. `block_counts`: some query block has all 16 entries live in every draw.
All inputs are finite; a program needn't handle non-finite values.
Results may differ from the reference program's by a relative error of at most 0.011.
Values may be sent and summed in bfloat16 or wider, within the bound.
No kernel may reach another device: no remote copies, remote signals or barrier semaphores. Data moves between devices by JAX's collectives and lax.ppermute only.
A program may use at most 64 MiB of HBM per device.

```python
import math
import jax
import jax.numpy as jnp
from jax import lax

D = 1024
HEADS = 16
HEAD = 64
BLK = 128
MAXNB = 16
NB = 16
NODES = 2048


def query_key_pair(key):
    query_seed = jax.random.fold_in(key, 11)
    key_seed = jax.random.fold_in(key, 12)
    key_vals = jnp.clip(jax.random.normal(key_seed, (NODES, D), jnp.float32), -6.0, 6.0)
    query_vals = jnp.clip(jax.random.normal(query_seed, (NODES, D), jnp.float32), -6.0, 6.0)
    return (query_vals, key_vals)


def draw_queries(key, part):
    return query_key_pair(key)[0].astype(jnp.bfloat16)


def draw_keys(key, part):
    return query_key_pair(key)[1].astype(jnp.bfloat16)


def draw_block_lists(key, part):
    list_seed = jax.random.fold_in(key, 21)
    rows = jnp.arange(NB, dtype=jnp.int32)[:, None]
    cols = jnp.arange(NB, dtype=jnp.int32)[None, :]
    ahead = (cols - rows) % NB
    distance = jnp.minimum(ahead, NB - ahead)
    noise = jax.random.randint(list_seed, (NB, NB), 0, 4 * NB, dtype=jnp.int32)
    score = (noise + distance) * NB + cols
    score = jnp.where(distance == 0, -1, score)
    order = jnp.argsort(score, axis=1, stable=True)
    return order[:, :MAXNB].astype(jnp.int32)


def draw_block_counts(key, part):
    first = jax.random.randint(jax.random.fold_in(key, 1), (NB,), 0, MAXNB, dtype=jnp.int32)
    second = jax.random.randint(jax.random.fold_in(key, 2), (NB,), 0, MAXNB, dtype=jnp.int32)
    counts = jnp.minimum(2 + first * second // MAXNB, MAXNB)
    peak = jax.random.randint(jax.random.fold_in(key, 3), (), 0, NB, dtype=jnp.int32)
    return jnp.where(jnp.arange(NB, dtype=jnp.int32) == peak, MAXNB, counts).astype(jnp.int32)


def shard_levels(rng, extent, split, least, top_value):
    level = 1.0
    for position, blocks in split:
        draws = jax.random.uniform(jax.random.fold_in(jax.random.fold_in(rng, 6), position), (blocks,), jnp.float32, least / len(split), top_value / len(split))
        level = level * jnp.repeat(jnp.exp(draws), extent[position] // blocks).reshape((-1,) + (1,) * (len(extent) - 1 - position))
    return level


def gaussian(rng, shape, width, most, shards=(), kind=jnp.bfloat16):
    loudness = shard_levels(rng, shape, shards, -0.22, 0.18) if shards else 1.0
    result = jax.random.normal(rng, shape, jnp.float32) * width * loudness
    return jnp.minimum(jnp.maximum(result, -most), most).astype(kind)


def setup_inputs(seed: int = 0, part: int = 0) -> dict:
    splits = jax.random.split(jax.random.key(seed), 7)
    own_keys = jax.random.split(jax.random.fold_in(splits[6], part), 7)
    queries = draw_queries(jax.random.fold_in(jax.random.fold_in(splits[6], part), 71), part)
    keys = draw_keys(jax.random.fold_in(jax.random.fold_in(splits[6], part), 71), part)
    values = gaussian(own_keys[2], (NODES, D), 1.0, 6.0, ((0, 4), (1, 4)))
    cotangent = gaussian(own_keys[3], (NODES, D), 1.0, 6.0, ((0, 4), (1, 4)))
    block_lists = draw_block_lists(jax.random.fold_in(jax.random.fold_in(splits[6], part), 71), part)
    block_counts = draw_block_counts(jax.random.fold_in(jax.random.fold_in(splits[6], part), 71), part)
    return {"queries": queries, "keys": keys, "values": values, "cotangent": cotangent, "block_lists": block_lists, "block_counts": block_counts}


def reference(queries, keys, values, cotangent, block_lists, block_counts):
    score_scale = 1.0 / math.sqrt(HEAD)
    slots = jnp.arange(MAXNB, dtype=jnp.int32)
    live_slots = slots[None, :] < block_counts[:, None]
    key_blocks = keys.reshape(NB, BLK, HEADS, HEAD)
    value_blocks = values.reshape(NB, BLK, HEADS, HEAD)
    query_blocks = queries.reshape(NB, BLK, HEADS, HEAD)
    grad_blocks = cotangent.reshape(NB, BLK, HEADS, HEAD)

    def gathered(table, chosen):
        return table[chosen].reshape(MAXNB * BLK, HEADS, HEAD).astype(jnp.float32)

    def probabilities(index):
        chosen = block_lists[index]
        keep_mask = jnp.repeat(live_slots[index], BLK)[None, None, :]
        key_rows = gathered(key_blocks, chosen)
        query_rows = query_blocks[index].astype(jnp.float32)
        scores = jnp.einsum('qhd,khd->hqk', query_rows, key_rows) * score_scale
        scores = jnp.where(keep_mask, scores, -1e+30)
        row_max = lax.optimization_barrier(jnp.max(scores, axis=2, keepdims=True))
        exp_terms = jnp.where(keep_mask, jnp.exp(scores - row_max), 0.0)
        weights = (exp_terms / lax.optimization_barrier(jnp.sum(exp_terms, axis=2, keepdims=True))).astype(jnp.bfloat16)
        weights = lax.optimization_barrier(weights).astype(jnp.float32)
        return (weights, chosen, key_rows, query_rows)

    def forward(index):
        weights, chosen, key_rows, query_rows = probabilities(index)
        value_rows = gathered(value_blocks, chosen)
        mixed = jnp.einsum('hqk,khd->qhd', weights, value_rows)
        return mixed.reshape(BLK, D).astype(jnp.bfloat16)
    attended = lax.map(forward, jnp.arange(NB, dtype=jnp.int32)).reshape(NODES, D)
    out_blocks = attended.reshape(NB, BLK, HEADS, HEAD)

    def backward(carry, index):
        key_accum, value_accum = carry
        weights, chosen, key_rows, query_rows = probabilities(index)
        value_rows = gathered(value_blocks, chosen)
        grad_rows = grad_blocks[index].astype(jnp.float32)
        delta = jnp.einsum('qhd,qhd->hq', grad_rows, out_blocks[index].astype(jnp.float32))
        dweights = jnp.einsum('qhd,khd->hqk', grad_rows, value_rows)
        dscores = (weights * (dweights - delta[:, :, None])).astype(jnp.bfloat16)
        dscores = lax.optimization_barrier(dscores).astype(jnp.float32)
        grad_query = score_scale * jnp.einsum('hqk,khd->qhd', dscores, key_rows)
        grad_key = score_scale * jnp.einsum('hqk,qhd->khd', dscores, query_rows)
        grad_value = jnp.einsum('hqk,qhd->khd', weights, grad_rows)
        key_accum = key_accum.at[chosen].add(grad_key.reshape(MAXNB, BLK, D))
        value_accum = value_accum.at[chosen].add(grad_value.reshape(MAXNB, BLK, D))
        return ((key_accum, value_accum), grad_query.reshape(BLK, D).astype(jnp.bfloat16))
    zeros_init = jnp.zeros((NB, BLK, D), jnp.float32)
    (key_accum, value_accum), grad_queries = lax.scan(backward, (zeros_init, zeros_init), jnp.arange(NB, dtype=jnp.int32))
    grad_queries = grad_queries.reshape(NODES, D)
    grad_keys = key_accum.reshape(NODES, D).astype(jnp.bfloat16)
    grad_values = value_accum.reshape(NODES, D).astype(jnp.bfloat16)
    return (attended, grad_queries, grad_keys, grad_values)
```

```python
import math

import jax
import jax.numpy as jnp
from jax import lax
from jax.experimental import pallas as pl
from jax.experimental.pallas import tpu as pltpu
from jax.sharding import PartitionSpec as P

D = 1024
HEADS = 16
HEAD = 64
BLK = 128
MAXNB = 16


NEG_FILL = -1e30
GROUP = 2
VMEM = pl.BlockSpec(memory_space=pltpu.VMEM)
SMEM = pl.BlockSpec(memory_space=pltpu.SMEM)


def pack_body(place, q_ref, g_ref, k_ref, v_ref, *outs):
    chunks = q_ref.shape[1] // HEAD

    def pack(left_ref, right_ref, out_refs, at):
        for step in range(chunks):
            head = (at + step) % chunks
            lanes = slice(head * HEAD, (head + 1) * HEAD)
            out_refs[step][...] = jnp.concatenate([left_ref[:, lanes], right_ref[:, lanes]], axis=1)

    for at in range(chunks):

        @pl.when(place[1] == at)
        def _():
            pack(k_ref, v_ref, outs[chunks:], at)

        @pl.when(place[0] == at)
        def _():
            pack(q_ref, g_ref, outs[:chunks], at)


def unpack_body(place, *refs):
    left_ref, right_ref = refs[-2:]
    chunks = len(refs) - 2
    for at in range(chunks):

        @pl.when(place[0] == at)
        def _():
            parts = [refs[(head - at) % chunks][...] for head in range(chunks)]
            left_ref[...] = jnp.concatenate([p[:, :HEAD] for p in parts], axis=1)
            right_ref[...] = jnp.concatenate([p[:, HEAD:] for p in parts], axis=1)


def attend_body(q_blocks, last, table, x_ref, *refs):
    kv_count = 4
    kv_refs = refs[:kv_count]
    acc_in = refs[kv_count]
    og_ref, acc_ref, kv_all, kvt, tiles = refs[kv_count + 1 :]
    scale = 1.0 / math.sqrt(HEAD)
    to_log2 = scale * math.log2(math.e)
    rows = kv_refs[0].shape[0]
    per_chunk = rows // BLK

    for part in range(kv_count):
        kv_all[part * rows : (part + 1) * rows, :] = kv_refs[part][...]
        for b in range(per_chunk):
            lanes = slice((part * per_chunk + b) * BLK, (part * per_chunk + b + 1) * BLK)
            kvt[:, lanes] = kv_refs[part][b * BLK : (b + 1) * BLK, :].T
    acc_ref[...] = acc_in[...]
    lane = lax.broadcasted_iota(jnp.int32, (BLK, 2 * HEAD), 1)
    is_left = lane < HEAD

    def fold(x, op):
        return op(x.reshape(x.shape[0] // 8, 8, x.shape[1]), axis=0)

    def query_block(qb, _):
        count = table[qb, MAXNB]
        groups = (count + GROUP - 1) // GROUP
        x = x_ref[pl.ds(pl.multiple_of(qb * BLK, BLK), BLK), :]
        zero = jnp.zeros_like(x)
        both = jnp.concatenate([jnp.where(is_left, x, zero), jnp.where(is_left, zero, x)], axis=0)

        def slot(at):
            return pl.multiple_of(table[qb, jnp.minimum(at, MAXNB - 1)] * BLK, BLK)

        def score_step(g, top):
            for u in range(GROUP):
                at = g * GROUP + u
                kv = kv_all[pl.ds(slot(at), BLK), :]
                st = lax.dot_general(
                    kv, both, (((1,), (1,)), ((), ())), preferred_element_type=jnp.float32
                )
                bias = jnp.where(at < count, 0.0, NEG_FILL)
                score = st[:, :BLK] * to_log2 + bias
                tiles[at, :, :BLK] = score
                tiles[at, :, BLK:] = st[:, BLK:]
                top = jnp.maximum(top, fold(score, jnp.max))
            return top

        top = lax.fori_loop(0, groups, score_step, jnp.full((8, BLK), NEG_FILL, jnp.float32))
        top = jnp.max(top, axis=0, keepdims=True)

        def exp_step(g, carry):
            total, dot = carry
            for u in range(GROUP):
                at = g * GROUP + u
                e = jnp.exp2(tiles[at, :, :BLK] - top)
                tiles[at, :, :BLK] = e
                total = total + fold(e, jnp.sum)
                dot = dot + fold(e * tiles[at, :, BLK:], jnp.sum)
            return total, dot

        zeros = jnp.zeros((8, BLK), jnp.float32)
        total, dot = lax.fori_loop(0, groups, exp_step, (zeros, zeros))
        inverse = 1.0 / jnp.sum(total, axis=0, keepdims=True)
        delta = jnp.sum(dot, axis=0, keepdims=True) * inverse

        def grad_step(g, out):
            for u in range(GROUP):
                at = g * GROUP + u
                w = tiles[at, :, :BLK] * inverse
                ds = (w * (tiles[at, :, BLK:] - delta)).astype(jnp.bfloat16)
                w = w.astype(jnp.bfloat16)
                start = slot(at)
                acc_ref[pl.ds(start, BLK), :] += jnp.dot(
                    jnp.concatenate([ds, w], axis=1), both, preferred_element_type=jnp.float32
                )
                t = kvt[:, pl.ds(start, BLK)]
                out = out + jnp.concatenate(
                    [
                        jnp.dot(t[HEAD:, :], w, preferred_element_type=jnp.float32),
                        jnp.dot(t[:HEAD, :], ds, preferred_element_type=jnp.float32) * scale,
                    ],
                    axis=0,
                )
            return out

        out = lax.fori_loop(0, groups, grad_step, jnp.zeros((2 * HEAD, BLK), jnp.float32))
        og_ref[pl.ds(pl.multiple_of(qb * BLK, BLK), BLK), :] = out.T.astype(og_ref.dtype)
        return 0

    lax.fori_loop(0, q_blocks, query_block, 0)


def gkv_round(acc, chunks):
    scale = 1.0 / math.sqrt(HEAD)
    lane = lax.broadcasted_iota(jnp.int32, acc.shape, 1)
    out = jnp.where(lane < HEAD, acc * scale, acc).astype(jnp.bfloat16)
    return out.reshape(chunks, -1, 2 * HEAD)


def head_per_device(queries, keys, values, cotangent, block_lists, block_counts):
    chunks = 4
    rows = queries.shape[0]
    q_blocks = rows // BLK
    at_row, at_col = lax.axis_index("row"), lax.axis_index("col")
    place = jnp.stack([at_row, at_col]).astype(jnp.int32)
    chunk = jax.ShapeDtypeStruct((rows, 2 * HEAD), jnp.bfloat16)
    packed = pl.pallas_call(
        pack_body,
        out_shape=[chunk] * (2 * chunks),
        in_specs=[SMEM] + [VMEM] * 4,
        out_specs=[VMEM] * (2 * chunks),
    )(place, queries, cotangent, keys, values)

    table = jnp.concatenate([block_lists, block_counts[:, None]], axis=1)

    def q_perm(step):
        return [
            (r * chunks + c, c * chunks + (r + step) % chunks)
            for r in range(chunks)
            for c in range(chunks)
        ]

    def k_perm(step):
        return [(c, (c + step) % chunks) for c in range(chunks)]

    def swap(perm):
        return [(b, a) for a, b in perm]

    axes = ("row", "col")
    kv = [packed[chunks]] + [
        lax.ppermute(packed[chunks + s], "col", k_perm(s)) for s in range(1, chunks)
    ]
    tables = [lax.ppermute(table, axes, q_perm(s)) for s in range(chunks)]
    xs = [lax.ppermute(packed[s], axes, q_perm(s)) for s in range(chunks)]

    acc = jnp.zeros((chunks * rows, 2 * HEAD), jnp.float32)
    outs = []
    for s in range(chunks):
        own = tables[s]
        block = own[:, :MAXNB]
        part = (at_col - block // q_blocks) % chunks
        slots = part * q_blocks + block % q_blocks
        own = jnp.concatenate([slots, own[:, MAXNB:]], axis=1)
        og, acc = pl.pallas_call(
            lambda *refs: attend_body(q_blocks, s == chunks - 1, *refs),
            out_shape=[chunk, jax.ShapeDtypeStruct(acc.shape, jnp.float32)],
            in_specs=[SMEM] + [VMEM] * (2 + chunks),
            out_specs=[VMEM, VMEM],
            scratch_shapes=[
                pltpu.VMEM((chunks * rows, 2 * HEAD), jnp.bfloat16),
                pltpu.VMEM((2 * HEAD, chunks * rows), jnp.bfloat16),
                pltpu.VMEM((MAXNB, BLK, 2 * BLK), jnp.float32),
            ],
            input_output_aliases={2 + chunks: 1},
        )(own, xs[s], *kv, acc)
        outs.append(lax.ppermute(og, axes, swap(q_perm(s))))
    gkv = gkv_round(acc, chunks)
    gkv = [gkv[0]] + [lax.ppermute(gkv[s], "col", swap(k_perm(s))) for s in range(1, chunks)]

    whole = jax.ShapeDtypeStruct(queries.shape, jnp.bfloat16)

    def unpack(at, parts):
        return pl.pallas_call(
            unpack_body,
            out_shape=[whole, whole],
            in_specs=[SMEM] + [VMEM] * chunks,
            out_specs=[VMEM, VMEM],
        )(jnp.reshape(at, (1,)).astype(jnp.int32), *parts)

    attended, grad_queries = unpack(at_row, outs)
    grad_keys, grad_values = unpack(at_col, gkv)
    return attended, grad_queries, grad_keys, grad_values


def tile_scores(query_tile, key_tile, score_scale):
    query_heads = query_tile.reshape(query_tile.shape[0], HEADS, -1)
    key_heads = key_tile.reshape(key_tile.shape[0], HEADS, -1)
    return (
        jnp.einsum("qhd,khd->hqk", query_heads, key_heads, preferred_element_type=jnp.float32)
        * score_scale
    )


def on_device(queries, keys, values, cotangent, block_lists, block_counts):
    score_scale = 1.0 / math.sqrt(HEAD)
    q_full = lax.all_gather(queries, "col", axis=1, tiled=True)
    k_full, v_full = (
        lax.all_gather(keys, "row", axis=1, tiled=True),
        lax.all_gather(values, "row", axis=1, tiled=True),
    )
    q_rows = q_full.shape[0]
    k_rows = k_full.shape[0]
    q_blocks = q_rows // BLK
    k_blocks = k_rows // BLK
    group_size = min(4, q_blocks)
    span_rows = group_size * BLK
    supers = q_blocks // group_size
    tile_count = supers * k_blocks
    first_key = lax.axis_index("col") * k_blocks
    wanted = first_key + jnp.arange(k_blocks, dtype=jnp.int32)
    live_slots = jnp.arange(MAXNB, dtype=jnp.int32)[None, :] < block_counts[:, None]
    block_hit = jnp.any(
        (block_lists[:, :, None] == wanted[None, None, :]) & live_slots[:, :, None], axis=1
    )
    block_hit = block_hit.reshape(supers, group_size, k_blocks).transpose(0, 2, 1)
    row_mask = jnp.repeat(block_hit, BLK, axis=2)
    tile_any = jnp.any(block_hit, axis=2)

    def tile_parts(step):
        super_at = step // k_blocks
        key_at = step % k_blocks
        query_tile = lax.dynamic_slice_in_dim(q_full, super_at * span_rows, span_rows, 0)
        key_tile = lax.dynamic_slice_in_dim(k_full, key_at * BLK, BLK, 0)
        value_tile = lax.dynamic_slice_in_dim(v_full, key_at * BLK, BLK, 0)
        keep_mask = row_mask[super_at, key_at][None, :, None]
        return (super_at, key_at, query_tile, key_tile, value_tile, keep_mask)

    def unchanged(carry):
        return carry

    def stats_step(step, carry):
        super_at, key_at, query_tile, key_tile, value_tile, keep_mask = tile_parts(step)

        def stats_work(state):
            row_top, row_total = state
            scores = jnp.where(keep_mask, tile_scores(query_tile, key_tile, score_scale), NEG_FILL)
            old_top = lax.dynamic_slice_in_dim(row_top, super_at * span_rows, span_rows, 1)
            old_total = lax.dynamic_slice_in_dim(row_total, super_at * span_rows, span_rows, 1)
            new_top = jnp.maximum(old_top, jnp.max(scores, axis=2))
            exp_terms = jnp.where(keep_mask, jnp.exp(scores - new_top[:, :, None]), 0.0)
            fresh = old_total * jnp.exp(old_top - new_top) + jnp.sum(exp_terms, axis=2)
            return (
                lax.dynamic_update_slice_in_dim(row_top, new_top, super_at * span_rows, 1),
                lax.dynamic_update_slice_in_dim(row_total, fresh, super_at * span_rows, 1),
            )

        return lax.cond(tile_any[super_at, key_at], stats_work, unchanged, carry)

    start_top = jnp.full((HEADS, q_rows), NEG_FILL, jnp.float32)
    start_total = jnp.zeros((HEADS, q_rows), jnp.float32)
    local_top, local_total = lax.fori_loop(0, tile_count, stats_step, (start_top, start_total))
    row_top = lax.pmax(local_top.astype(jnp.bfloat16), "col").astype(local_top.dtype)
    row_total = lax.psum(local_total * jnp.exp(local_top - row_top), "col")

    def tile_weights(scores, super_at, keep_mask):
        top_rows = lax.dynamic_slice_in_dim(row_top, super_at * span_rows, span_rows, 1)
        total_rows = lax.dynamic_slice_in_dim(row_total, super_at * span_rows, span_rows, 1)
        ratio = jnp.exp(scores - top_rows[:, :, None]) / total_rows[:, :, None]
        return jnp.where(keep_mask, ratio, 0.0).astype(jnp.bfloat16)

    def output_step(step, carry):
        super_at, key_at, query_tile, key_tile, value_tile, keep_mask = tile_parts(step)

        def output_work(out_rows):
            scores = jnp.where(keep_mask, tile_scores(query_tile, key_tile, score_scale), NEG_FILL)
            weights = tile_weights(scores, super_at, keep_mask)
            value_heads = value_tile.reshape(BLK, HEADS, -1)
            part = jnp.einsum(
                "hqk,khd->qhd", weights, value_heads, preferred_element_type=jnp.float32
            ).reshape(span_rows, -1)
            current = lax.dynamic_slice_in_dim(out_rows, super_at * span_rows, span_rows, 0)
            return lax.dynamic_update_slice_in_dim(
                out_rows, current + part, super_at * span_rows, 0
            )

        return lax.cond(tile_any[super_at, key_at], output_work, unchanged, carry)

    partial_out = lax.fori_loop(0, tile_count, output_step, jnp.zeros((q_rows, D), jnp.float32))
    out_share = lax.psum_scatter(partial_out, "col", scatter_dimension=1, tiled=True).astype(
        jnp.bfloat16
    )
    grad_full, out_full = (
        lax.all_gather(cotangent, "col", axis=1, tiled=True),
        lax.all_gather(out_share, "col", axis=1, tiled=True),
    )
    delta = jnp.einsum(
        "qhd,qhd->hq",
        grad_full.reshape(q_rows, HEADS, -1),
        out_full.reshape(q_rows, HEADS, -1),
        preferred_element_type=jnp.float32,
    )

    def grad_step(step, carry):
        super_at, key_at, query_tile, key_tile, value_tile, keep_mask = tile_parts(step)

        def grad_work(state):
            query_accum, key_accum, value_accum = state
            scores = jnp.where(keep_mask, tile_scores(query_tile, key_tile, score_scale), NEG_FILL)
            weights = tile_weights(scores, super_at, keep_mask)
            grad_tile = lax.dynamic_slice_in_dim(
                grad_full, super_at * span_rows, span_rows, 0
            ).reshape(span_rows, HEADS, -1)
            value_heads = value_tile.reshape(BLK, HEADS, -1)
            key_heads = key_tile.reshape(BLK, HEADS, -1)
            query_heads = query_tile.reshape(span_rows, HEADS, -1)
            dweights = jnp.einsum(
                "qhd,khd->hqk", grad_tile, value_heads, preferred_element_type=jnp.float32
            )
            delta_rows = lax.dynamic_slice_in_dim(delta, super_at * span_rows, span_rows, 1)
            dscores = (weights.astype(jnp.float32) * (dweights - delta_rows[:, :, None])).astype(
                jnp.bfloat16
            )
            query_part = score_scale * jnp.einsum(
                "hqk,khd->qhd", dscores, key_heads, preferred_element_type=jnp.float32
            )
            key_part = score_scale * jnp.einsum(
                "hqk,qhd->khd", dscores, query_heads, preferred_element_type=jnp.float32
            )
            value_part = jnp.einsum(
                "hqk,qhd->khd", weights, grad_tile, preferred_element_type=jnp.float32
            )
            query_now = lax.dynamic_slice_in_dim(query_accum, super_at * span_rows, span_rows, 0)
            key_now = lax.dynamic_slice_in_dim(key_accum, key_at * BLK, BLK, 0)
            value_now = lax.dynamic_slice_in_dim(value_accum, key_at * BLK, BLK, 0)
            query_accum = lax.dynamic_update_slice_in_dim(
                query_accum, query_now + query_part.reshape(span_rows, -1), super_at * span_rows, 0
            )
            key_accum = lax.dynamic_update_slice_in_dim(
                key_accum, key_now + key_part.reshape(BLK, -1), key_at * BLK, 0
            )
            value_accum = lax.dynamic_update_slice_in_dim(
                value_accum, value_now + value_part.reshape(BLK, -1), key_at * BLK, 0
            )
            return (query_accum, key_accum, value_accum)

        return lax.cond(tile_any[super_at, key_at], grad_work, unchanged, carry)

    start_grads = (
        jnp.zeros((q_rows, D), jnp.float32),
        jnp.zeros((k_rows, D), jnp.float32),
        jnp.zeros((k_rows, D), jnp.float32),
    )
    query_parts, key_parts, value_parts = lax.fori_loop(0, tile_count, grad_step, start_grads)
    grad_queries = lax.psum_scatter(query_parts, "col", scatter_dimension=1, tiled=True).astype(
        jnp.bfloat16
    )
    grad_keys, grad_values = (
        lax.psum_scatter(key_parts, "row", scatter_dimension=1, tiled=True),
        lax.psum_scatter(value_parts, "row", scatter_dimension=1, tiled=True),
    )
    return (
        out_share,
        grad_queries,
        grad_keys.astype(jnp.bfloat16),
        grad_values.astype(jnp.bfloat16),
    )


def solution(mesh):
    rows, cols = mesh.shape["row"], mesh.shape["col"]
    one_head = rows == 4 and cols == 4
    return jax.shard_map(
        head_per_device if one_head else on_device,
        mesh=mesh,
        in_specs=(
            P(("groups", "row"), "col"),
            P(("groups", "col"), "row"),
            P(("groups", "col"), "row"),
            P(("groups", "row"), "col"),
            P(("groups", "row"), None),
            P(("groups", "row")),
        ),
        out_specs=(
            P(("groups", "row"), "col"),
            P(("groups", "row"), "col"),
            P(("groups", "col"), "row"),
            P(("groups", "col"), "row"),
        ),
        check_vma=False,
    )
```

```python
import functools
import math

import jax
import jax.numpy as jnp
from jax import lax
from jax.experimental import pallas as pl
from jax.experimental.pallas import tpu as pltpu
from jax.sharding import PartitionSpec as P

D = 1024
HEADS = 16
HEAD = 64
BLK = 128
MAXNB = 16


NEG_FILL = -1e30
GROUP = 4
STREAMS = 4
TAIL = 16
VMEM = pl.BlockSpec(memory_space=pltpu.VMEM)
SMEM = pl.BlockSpec(memory_space=pltpu.SMEM)


def pack_body(place, lists, counts, q_ref, g_ref, k_ref, v_ref, *outs):
    chunks = q_ref.shape[1] // HEAD
    rows = q_ref.shape[0]

    def pack(left_ref, right_ref, out_refs, at):
        for step in range(chunks):
            head = (at + step) % chunks
            lanes = slice(head * HEAD, (head + 1) * HEAD)
            out_refs[step][:rows, :] = jnp.concatenate(
                [left_ref[:, lanes], right_ref[:, lanes]], axis=1
            )

    for at in range(chunks):

        @pl.when(place[1] == at)
        def _():
            pack(k_ref, v_ref, outs[chunks:], at)

        @pl.when(place[0] == at)
        def _():
            pack(q_ref, g_ref, outs[:chunks], at)

    row = lax.broadcasted_iota(jnp.int32, (TAIL, 2 * HEAD), 0)
    lane = lax.broadcasted_iota(jnp.int32, (TAIL, 2 * HEAD), 1)
    table = jnp.zeros((TAIL, 2 * HEAD), jnp.int32)
    for qb in range(rows // BLK):
        line = jnp.where(lane == MAXNB, counts[qb], 0)
        for at in range(MAXNB):
            line = jnp.where(lane == at, lists[qb, at], line)
        table = jnp.where(row == qb, line, table)
    table = table.astype(jnp.float32).astype(jnp.bfloat16)
    for out_ref in outs[:chunks]:
        out_ref[rows:, :] = table


def unpack_body(place, *refs):
    left_ref, right_ref = refs[-2:]
    chunks = len(refs) - 2
    for at in range(chunks):

        @pl.when(place[0] == at)
        def _():
            parts = [refs[(head - at) % chunks][...] for head in range(chunks)]
            left_ref[...] = jnp.concatenate([p[:, :HEAD] for p in parts], axis=1)
            right_ref[...] = jnp.concatenate([p[:, HEAD:] for p in parts], axis=1)


def fold(x, op):
    return op(x.reshape(x.shape[0] // 8, 8, x.shape[1]), axis=0)


def attend_body(chunks, place, *refs):
    x_refs, kv_refs = refs[:chunks], refs[chunks : 2 * chunks]
    og_refs, gkv_refs = refs[2 * chunks : 3 * chunks], refs[3 * chunks : 4 * chunks]
    (x_all, kv_all, wide, table, items, both, both_t, kv_t, stat, tiles, tops) = refs[
        4 * chunks : 4 * chunks + 11
    ]
    rest = refs[4 * chunks + 11 :]
    sem, table_sem = rest[:2]
    rest = rest[2:]
    accs, outs, stats = rest[:STREAMS], rest[STREAMS : 2 * STREAMS], rest[2 * STREAMS :]
    scale = 1.0 / math.sqrt(HEAD)
    to_log2 = scale * math.log2(math.e)
    rows = kv_refs[0].shape[0]
    per_chunk = rows // BLK
    blocks = chunks * per_chunk

    copies = []
    for c in range(chunks):
        copies.append(pltpu.make_async_copy(x_refs[c], x_all.at[c], sem.at[c]))
        copies.append(
            pltpu.make_async_copy(
                kv_refs[c], kv_all.at[pl.ds(c * rows, rows), :], sem.at[chunks + c]
            )
        )
    for copy in copies:
        copy.start()
    for s in range(STREAMS):
        accs[s][...] = jnp.zeros_like(accs[s])
        outs[s][...] = jnp.zeros_like(outs[s])
        stats[s][0] = jnp.full(stats[s].shape[1:], NEG_FILL, jnp.float32)
        stats[s][1] = jnp.zeros(stats[s].shape[1:], jnp.float32)
        stats[s][2] = jnp.zeros(stats[s].shape[1:], jnp.float32)
    for copy in copies:
        copy.wait()

    lane = lax.broadcasted_iota(jnp.int32, (TAIL, 2 * HEAD), 1)
    for c in range(chunks):
        listed = x_all[c, rows:, :].astype(jnp.float32).astype(jnp.int32)
        part = lax.rem(place[1] - lax.div(listed, per_chunk) + chunks, chunks)
        slot = part * per_chunk + lax.rem(listed, per_chunk)
        wide[c * TAIL : (c + 1) * TAIL, :] = jnp.where(lane < MAXNB, slot, listed)
    copy = pltpu.make_async_copy(wide, table, table_sem)
    copy.start()

    is_left = lax.broadcasted_iota(jnp.int32, (BLK, 2 * HEAD), 1) < HEAD
    zeros = jnp.zeros((HEAD, BLK), jnp.bfloat16)
    for b in range(blocks):
        kv_t[:, b * BLK : (b + 1) * BLK] = kv_all[b * BLK : (b + 1) * BLK, :].T
        at = (b % per_chunk) * BLK
        x = x_all[b // per_chunk, at : at + BLK, :]
        both[b, :BLK, :] = jnp.where(is_left, x, jnp.zeros_like(x))
        both[b, BLK:, :] = jnp.where(is_left, jnp.zeros_like(x), x)
        x_t = x.T
        both_t[b, :HEAD, :BLK] = x_t[:HEAD]
        both_t[b, :HEAD, BLK:] = zeros
        both_t[b, HEAD:, :BLK] = zeros
        both_t[b, HEAD:, BLK:] = x_t[HEAD:]
    copy.wait()

    def line(qb):
        return lax.div(qb, per_chunk) * TAIL + lax.rem(qb, per_chunk)

    def add_items(qb, count):
        groups = (table[line(qb), MAXNB] + GROUP - 1) // GROUP

        def add_item(g, _):
            items[0, count + g] = qb
            items[1, count + g] = g * GROUP
            return 0

        lax.fori_loop(0, groups, add_item, 0)
        return count + groups

    count = lax.fori_loop(0, blocks, add_items, 0)
    steps = (count + STREAMS - 1) // STREAMS
    for s in range(STREAMS - 1):
        items[0, count + s] = 0
        items[1, count + s] = MAXNB

    def item(at):
        qb, base = items[0, at], items[1, at]
        slots = [
            pl.multiple_of(table[line(qb), jnp.minimum(base + u, MAXNB - 1)] * BLK, BLK)
            for u in range(GROUP)
        ]
        return qb, base, slots

    def score_step(i, _):
        for s in range(STREAMS):
            at = s * steps + i
            qb, base, slots = item(at)
            live = table[line(qb), MAXNB]
            kv = jnp.concatenate([kv_all[pl.ds(k, BLK), :] for k in slots], axis=0)
            both_scores = jnp.dot(kv, both_t[qb], preferred_element_type=jnp.float32)
            scores = [
                both_scores[u * BLK : (u + 1) * BLK, :BLK] * to_log2
                + jnp.where(base + u < live, 0.0, NEG_FILL)
                for u in range(GROUP)
            ]
            top = functools.reduce(jnp.maximum, [fold(v, jnp.max) for v in scores])
            top = jnp.max(top, axis=0, keepdims=True)
            total = jnp.zeros((8, BLK), jnp.float32)
            dot = jnp.zeros((8, BLK), jnp.float32)
            for u in range(GROUP):
                part = slice(u * BLK, (u + 1) * BLK)
                e = jnp.exp2(scores[u] - top)
                dw = both_scores[part, BLK:]
                tiles[at, part, :BLK] = e
                tiles[at, part, BLK:] = dw
                total = total + fold(e, jnp.sum)
                dot = dot + fold(e * dw, jnp.sum)
            total = jnp.sum(total, axis=0, keepdims=True)
            dot = jnp.sum(dot, axis=0, keepdims=True)
            tops[pl.ds(at, 1), :] = top
            row = pl.ds(qb, 1)
            old = stats[s][0, row, :]
            new = jnp.maximum(old, top)
            old_part, new_part = jnp.exp2(old - new), jnp.exp2(top - new)
            stats[s][0, row, :] = new
            stats[s][1, row, :] = stats[s][1, row, :] * old_part + total * new_part
            stats[s][2, row, :] = stats[s][2, row, :] * old_part + dot * new_part
        return 0

    lax.fori_loop(0, steps, score_step, 0)

    top = functools.reduce(jnp.maximum, [st[0] for st in stats])
    total = functools.reduce(jnp.add, [st[1] * jnp.exp2(st[0] - top) for st in stats])
    dot = functools.reduce(jnp.add, [st[2] * jnp.exp2(st[0] - top) for st in stats])
    stat[0] = top
    stat[1] = 1.0 / total
    stat[2] = dot / total

    def grad_step(i, _):
        for s in range(STREAMS):
            at = s * steps + i
            qb, base, slots = item(at)
            row = pl.ds(qb, 1)
            factor = stat[1, row, :] * jnp.exp2(tops[pl.ds(at, 1), :] - stat[0, row, :])
            delta = stat[2, row, :]
            w, ds = [], []
            for u in range(GROUP):
                part = slice(u * BLK, (u + 1) * BLK)
                weights = tiles[at, part, :BLK] * factor
                ds.append((weights * (tiles[at, part, BLK:] - delta)).astype(jnp.bfloat16))
                w.append(weights.astype(jnp.bfloat16))
            pair = jnp.concatenate(
                [jnp.concatenate(ds, axis=0), jnp.concatenate(w, axis=0)], axis=1
            )
            grads = jnp.dot(pair, both[qb], preferred_element_type=jnp.float32)
            for u in range(GROUP):
                accs[s][pl.ds(slots[u], BLK), :] += grads[u * BLK : (u + 1) * BLK]
            t = jnp.concatenate([kv_t[:, pl.ds(k, BLK)] for k in slots], axis=1)
            sums = jnp.dot(t, pair, preferred_element_type=jnp.float32)
            outs[s][qb, :HEAD, :] += sums[HEAD:, BLK:]
            outs[s][qb, HEAD:, :] += sums[:HEAD, :BLK]
        return 0

    lax.fori_loop(0, steps, grad_step, 0)

    is_out = lax.broadcasted_iota(jnp.int32, (2 * HEAD, BLK), 0) < HEAD
    for b in range(blocks):
        out = functools.reduce(jnp.add, [r[b] for r in outs])
        out = jnp.where(is_out, out, out * scale)
        at = (b % per_chunk) * BLK
        og_refs[b // per_chunk][at : at + BLK, :] = out.T.astype(jnp.bfloat16)
        acc = functools.reduce(jnp.add, [r[b * BLK : (b + 1) * BLK, :] for r in accs])
        acc = jnp.where(is_left, acc * scale, acc)
        gkv_refs[b // per_chunk][at : at + BLK, :] = acc.astype(jnp.bfloat16)


def in_vmem(x):
    return pltpu.with_memory_space_constraint(x, pltpu.VMEM)


def head_per_device(queries, keys, values, cotangent, block_lists, block_counts):
    chunks = 4
    rows = queries.shape[0]
    at_row, at_col = lax.axis_index("row"), lax.axis_index("col")
    place = jnp.stack([at_row, at_col]).astype(jnp.int32)
    chunk = pltpu.VMEM((rows, 2 * HEAD), jnp.bfloat16)
    tailed = pltpu.VMEM((rows + TAIL, 2 * HEAD), jnp.bfloat16)
    packed = pl.pallas_call(
        pack_body,
        out_shape=[tailed] * chunks + [chunk] * chunks,
        in_specs=[SMEM] * 3 + [VMEM] * 4,
        out_specs=[VMEM] * (2 * chunks),
        name="pack",
    )(place, block_lists, block_counts, queries, cotangent, keys, values)

    def q_perm(step):
        return [
            (r * chunks + c, c * chunks + (r + step) % chunks)
            for r in range(chunks)
            for c in range(chunks)
        ]

    def k_perm(step):
        return [(c, (c + step) % chunks) for c in range(chunks)]

    def swap(perm):
        return [(b, a) for a, b in perm]

    axes = ("row", "col")
    kv = [packed[chunks]] + [
        lax.ppermute(packed[chunks + s], "col", k_perm(s)) for s in range(1, chunks)
    ]
    xs = [lax.ppermute(packed[s], axes, q_perm(s)) for s in range(chunks)]

    blocks = chunks * rows // BLK
    most = blocks * MAXNB // GROUP + STREAMS
    results = pl.pallas_call(
        functools.partial(attend_body, chunks),
        out_shape=[chunk] * (2 * chunks),
        in_specs=[SMEM] + [VMEM] * (2 * chunks),
        out_specs=[VMEM] * (2 * chunks),
        scratch_shapes=[
            pltpu.VMEM((chunks, rows + TAIL, 2 * HEAD), jnp.bfloat16),
            pltpu.VMEM((chunks * rows, 2 * HEAD), jnp.bfloat16),
            pltpu.VMEM((chunks * TAIL, 2 * HEAD), jnp.int32),
            pltpu.SMEM((chunks * TAIL, 2 * HEAD), jnp.int32),
            pltpu.SMEM((2, most), jnp.int32),
            pltpu.VMEM((blocks, 2 * BLK, 2 * HEAD), jnp.bfloat16),
            pltpu.VMEM((blocks, 2 * HEAD, 2 * BLK), jnp.bfloat16),
            pltpu.VMEM((2 * HEAD, chunks * rows), jnp.bfloat16),
            pltpu.VMEM((3, blocks, BLK), jnp.float32),
            pltpu.VMEM((most, GROUP * BLK, 2 * BLK), jnp.float32),
            pltpu.VMEM((most, BLK), jnp.float32),
            pltpu.SemaphoreType.DMA((2 * chunks,)),
            pltpu.SemaphoreType.DMA,
        ]
        + [pltpu.VMEM((chunks * rows, 2 * HEAD), jnp.float32)] * STREAMS
        + [pltpu.VMEM((blocks, 2 * HEAD, BLK), jnp.float32)] * STREAMS
        + [pltpu.VMEM((3, blocks, BLK), jnp.float32)] * STREAMS,
        compiler_params=pltpu.CompilerParams(vmem_limit_bytes=56 * 1024 * 1024),
        name="attend",
    )(place, *[in_vmem(a) for a in (*xs, *kv)])
    ogs, gkv = results[:chunks], results[chunks:]
    ogs = [lax.ppermute(ogs[s], axes, swap(q_perm(s))) for s in range(chunks)]
    gkv = [gkv[0]] + [lax.ppermute(gkv[s], "col", swap(k_perm(s))) for s in range(1, chunks)]

    whole = jax.ShapeDtypeStruct(queries.shape, jnp.bfloat16)

    def unpack(at, parts):
        return pl.pallas_call(
            unpack_body,
            out_shape=[whole, whole],
            in_specs=[SMEM] + [VMEM] * chunks,
            out_specs=[VMEM, VMEM],
            name="unpack",
        )(jnp.reshape(at, (1,)).astype(jnp.int32), *[in_vmem(p) for p in parts])

    attended, grad_queries = unpack(at_row, ogs)
    grad_keys, grad_values = unpack(at_col, gkv)
    return attended, grad_queries, grad_keys, grad_values


def tile_scores(query_tile, key_tile, score_scale):
    query_heads = query_tile.reshape(query_tile.shape[0], HEADS, -1)
    key_heads = key_tile.reshape(key_tile.shape[0], HEADS, -1)
    return (
        jnp.einsum("qhd,khd->hqk", query_heads, key_heads, preferred_element_type=jnp.float32)
        * score_scale
    )


def on_device(queries, keys, values, cotangent, block_lists, block_counts):
    score_scale = 1.0 / math.sqrt(HEAD)
    q_full = lax.all_gather(queries, "col", axis=1, tiled=True)
    k_full, v_full = (
        lax.all_gather(keys, "row", axis=1, tiled=True),
        lax.all_gather(values, "row", axis=1, tiled=True),
    )
    q_rows = q_full.shape[0]
    k_rows = k_full.shape[0]
    q_blocks = q_rows // BLK
    k_blocks = k_rows // BLK
    group_size = min(4, q_blocks)
    span_rows = group_size * BLK
    supers = q_blocks // group_size
    tile_count = supers * k_blocks
    first_key = lax.axis_index("col") * k_blocks
    wanted = first_key + jnp.arange(k_blocks, dtype=jnp.int32)
    live_slots = jnp.arange(MAXNB, dtype=jnp.int32)[None, :] < block_counts[:, None]
    block_hit = jnp.any(
        (block_lists[:, :, None] == wanted[None, None, :]) & live_slots[:, :, None], axis=1
    )
    block_hit = block_hit.reshape(supers, group_size, k_blocks).transpose(0, 2, 1)
    row_mask = jnp.repeat(block_hit, BLK, axis=2)
    tile_any = jnp.any(block_hit, axis=2)

    def tile_parts(step):
        super_at = step // k_blocks
        key_at = step % k_blocks
        query_tile = lax.dynamic_slice_in_dim(q_full, super_at * span_rows, span_rows, 0)
        key_tile = lax.dynamic_slice_in_dim(k_full, key_at * BLK, BLK, 0)
        value_tile = lax.dynamic_slice_in_dim(v_full, key_at * BLK, BLK, 0)
        keep_mask = row_mask[super_at, key_at][None, :, None]
        return (super_at, key_at, query_tile, key_tile, value_tile, keep_mask)

    def unchanged(carry):
        return carry

    def stats_step(step, carry):
        super_at, key_at, query_tile, key_tile, value_tile, keep_mask = tile_parts(step)

        def stats_work(state):
            row_top, row_total = state
            scores = jnp.where(keep_mask, tile_scores(query_tile, key_tile, score_scale), NEG_FILL)
            old_top = lax.dynamic_slice_in_dim(row_top, super_at * span_rows, span_rows, 1)
            old_total = lax.dynamic_slice_in_dim(row_total, super_at * span_rows, span_rows, 1)
            new_top = jnp.maximum(old_top, jnp.max(scores, axis=2))
            exp_terms = jnp.where(keep_mask, jnp.exp(scores - new_top[:, :, None]), 0.0)
            fresh = old_total * jnp.exp(old_top - new_top) + jnp.sum(exp_terms, axis=2)
            return (
                lax.dynamic_update_slice_in_dim(row_top, new_top, super_at * span_rows, 1),
                lax.dynamic_update_slice_in_dim(row_total, fresh, super_at * span_rows, 1),
            )

        return lax.cond(tile_any[super_at, key_at], stats_work, unchanged, carry)

    start_top = jnp.full((HEADS, q_rows), NEG_FILL, jnp.float32)
    start_total = jnp.zeros((HEADS, q_rows), jnp.float32)
    local_top, local_total = lax.fori_loop(0, tile_count, stats_step, (start_top, start_total))
    row_top = lax.pmax(local_top.astype(jnp.bfloat16), "col").astype(local_top.dtype)
    row_total = lax.psum(local_total * jnp.exp(local_top - row_top), "col")

    def tile_weights(scores, super_at, keep_mask):
        top_rows = lax.dynamic_slice_in_dim(row_top, super_at * span_rows, span_rows, 1)
        total_rows = lax.dynamic_slice_in_dim(row_total, super_at * span_rows, span_rows, 1)
        ratio = jnp.exp(scores - top_rows[:, :, None]) / total_rows[:, :, None]
        return jnp.where(keep_mask, ratio, 0.0).astype(jnp.bfloat16)

    def output_step(step, carry):
        super_at, key_at, query_tile, key_tile, value_tile, keep_mask = tile_parts(step)

        def output_work(out_rows):
            scores = jnp.where(keep_mask, tile_scores(query_tile, key_tile, score_scale), NEG_FILL)
            weights = tile_weights(scores, super_at, keep_mask)
            value_heads = value_tile.reshape(BLK, HEADS, -1)
            part = jnp.einsum(
                "hqk,khd->qhd", weights, value_heads, preferred_element_type=jnp.float32
            ).reshape(span_rows, -1)
            current = lax.dynamic_slice_in_dim(out_rows, super_at * span_rows, span_rows, 0)
            return lax.dynamic_update_slice_in_dim(
                out_rows, current + part, super_at * span_rows, 0
            )

        return lax.cond(tile_any[super_at, key_at], output_work, unchanged, carry)

    partial_out = lax.fori_loop(0, tile_count, output_step, jnp.zeros((q_rows, D), jnp.float32))
    out_share = lax.psum_scatter(partial_out, "col", scatter_dimension=1, tiled=True).astype(
        jnp.bfloat16
    )
    grad_full, out_full = (
        lax.all_gather(cotangent, "col", axis=1, tiled=True),
        lax.all_gather(out_share, "col", axis=1, tiled=True),
    )
    delta = jnp.einsum(
        "qhd,qhd->hq",
        grad_full.reshape(q_rows, HEADS, -1),
        out_full.reshape(q_rows, HEADS, -1),
        preferred_element_type=jnp.float32,
    )

    def grad_step(step, carry):
        super_at, key_at, query_tile, key_tile, value_tile, keep_mask = tile_parts(step)

        def grad_work(state):
            query_accum, key_accum, value_accum = state
            scores = jnp.where(keep_mask, tile_scores(query_tile, key_tile, score_scale), NEG_FILL)
            weights = tile_weights(scores, super_at, keep_mask)
            grad_tile = lax.dynamic_slice_in_dim(
                grad_full, super_at * span_rows, span_rows, 0
            ).reshape(span_rows, HEADS, -1)
            value_heads = value_tile.reshape(BLK, HEADS, -1)
            key_heads = key_tile.reshape(BLK, HEADS, -1)
            query_heads = query_tile.reshape(span_rows, HEADS, -1)
            dweights = jnp.einsum(
                "qhd,khd->hqk", grad_tile, value_heads, preferred_element_type=jnp.float32
            )
            delta_rows = lax.dynamic_slice_in_dim(delta, super_at * span_rows, span_rows, 1)
            dscores = (weights.astype(jnp.float32) * (dweights - delta_rows[:, :, None])).astype(
                jnp.bfloat16
            )
            query_part = score_scale * jnp.einsum(
                "hqk,khd->qhd", dscores, key_heads, preferred_element_type=jnp.float32
            )
            key_part = score_scale * jnp.einsum(
                "hqk,qhd->khd", dscores, query_heads, preferred_element_type=jnp.float32
            )
            value_part = jnp.einsum(
                "hqk,qhd->khd", weights, grad_tile, preferred_element_type=jnp.float32
            )
            query_now = lax.dynamic_slice_in_dim(query_accum, super_at * span_rows, span_rows, 0)
            key_now = lax.dynamic_slice_in_dim(key_accum, key_at * BLK, BLK, 0)
            value_now = lax.dynamic_slice_in_dim(value_accum, key_at * BLK, BLK, 0)
            query_accum = lax.dynamic_update_slice_in_dim(
                query_accum, query_now + query_part.reshape(span_rows, -1), super_at * span_rows, 0
            )
            key_accum = lax.dynamic_update_slice_in_dim(
                key_accum, key_now + key_part.reshape(BLK, -1), key_at * BLK, 0
            )
            value_accum = lax.dynamic_update_slice_in_dim(
                value_accum, value_now + value_part.reshape(BLK, -1), key_at * BLK, 0
            )
            return (query_accum, key_accum, value_accum)

        return lax.cond(tile_any[super_at, key_at], grad_work, unchanged, carry)

    start_grads = (
        jnp.zeros((q_rows, D), jnp.float32),
        jnp.zeros((k_rows, D), jnp.float32),
        jnp.zeros((k_rows, D), jnp.float32),
    )
    query_parts, key_parts, value_parts = lax.fori_loop(0, tile_count, grad_step, start_grads)
    grad_queries = lax.psum_scatter(query_parts, "col", scatter_dimension=1, tiled=True).astype(
        jnp.bfloat16
    )
    grad_keys, grad_values = (
        lax.psum_scatter(key_parts, "row", scatter_dimension=1, tiled=True),
        lax.psum_scatter(value_parts, "row", scatter_dimension=1, tiled=True),
    )
    return (
        out_share,
        grad_queries,
        grad_keys.astype(jnp.bfloat16),
        grad_values.astype(jnp.bfloat16),
    )


def solution(mesh):
    rows, cols = mesh.shape["row"], mesh.shape["col"]
    one_head = rows == 4 and cols == 4
    return jax.shard_map(
        head_per_device if one_head else on_device,
        mesh=mesh,
        in_specs=(
            P(("groups", "row"), "col"),
            P(("groups", "col"), "row"),
            P(("groups", "col"), "row"),
            P(("groups", "row"), "col"),
            P(("groups", "row"), None),
            P(("groups", "row")),
        ),
        out_specs=(
            P(("groups", "row"), "col"),
            P(("groups", "row"), "col"),
            P(("groups", "col"), "row"),
            P(("groups", "col"), "row"),
        ),
        check_vma=False,
    )
```

```python
import functools
import math

import jax
import jax.numpy as jnp
from jax import lax
from jax.experimental import pallas as pl
from jax.experimental.pallas import tpu as pltpu
from jax.sharding import PartitionSpec as P

D = 1024
HEADS = 16
HEAD = 64
BLK = 128
MAXNB = 16


NEG_FILL = -1e30
GROUP = 4
STREAMS = 4
TAIL = 16
BATCHES = (1, 2, 1)
VMEM_LIMIT = 40 * 1024 * 1024
VMEM = pl.BlockSpec(memory_space=pltpu.VMEM)
SMEM = pl.BlockSpec(memory_space=pltpu.SMEM)


def pack_body(lists, counts, q_ref, g_ref, k_ref, v_ref, *outs):
    chunks = q_ref.shape[1] // HEAD
    rows = q_ref.shape[0]

    def pack(left_ref, right_ref, out_refs, at):
        for step in range(chunks):
            head = (at + step) % chunks
            lanes = slice(head * HEAD, (head + 1) * HEAD)
            out_refs[step][:rows, :] = jnp.concatenate(
                [left_ref[:, lanes], right_ref[:, lanes]], axis=1
            )

    for at in range(chunks):

        @pl.when(lax.axis_index("col") == at)
        def _():
            pack(k_ref, v_ref, outs[chunks:], at)

        @pl.when(lax.axis_index("row") == at)
        def _():
            pack(q_ref, g_ref, outs[:chunks], at)

    row = lax.broadcasted_iota(jnp.int32, (TAIL, 2 * HEAD), 0)
    lane = lax.broadcasted_iota(jnp.int32, (TAIL, 2 * HEAD), 1)
    table = jnp.zeros((TAIL, 2 * HEAD), jnp.int32)
    for qb in range(rows // BLK):
        line = jnp.where(lane == MAXNB, counts[qb], 0)
        for at in range(MAXNB):
            line = jnp.where(lane == at, lists[qb, at], line)
        table = jnp.where(row == qb, line, table)
    table = table.astype(jnp.float32).astype(jnp.bfloat16)
    for out_ref in outs[:chunks]:
        out_ref[rows:, :] = table


def unpack_body(axis, *refs):
    left_ref, right_ref = refs[-2:]
    chunks = len(refs) - 2
    for at in range(chunks):

        @pl.when(lax.axis_index(axis) == at)
        def _():
            parts = [refs[(head - at) % chunks][...] for head in range(chunks)]
            left_ref[...] = jnp.concatenate([p[:, :HEAD] for p in parts], axis=1)
            right_ref[...] = jnp.concatenate([p[:, HEAD:] for p in parts], axis=1)


def fold(x, op):
    return op(x.reshape(x.shape[0] // 8, 8, x.shape[1]), axis=0)


def attend_body(chunks, parts, first, last, *refs):
    def take(count):
        nonlocal refs
        head, refs = refs[:count], refs[count:]
        return head

    x_refs = take(chunks)
    if first:
        kv_refs = take(parts)
    else:
        kv_all, kv_t, acc_in = take(3)
    og_refs = take(chunks)
    if last:
        gkv_refs = take(parts)
    else:
        (acc_out,) = take(1)
    if first:
        kv_all, kv_t = take(2)
    wide, table, items, both, both_t, stat, tiles, tops, sem, table_sem = take(10)
    accs, outs, stats = take(STREAMS), take(STREAMS), take(STREAMS)
    scale = 1.0 / math.sqrt(HEAD)
    to_log2 = scale * math.log2(math.e)
    rows = kv_all.shape[0] // parts
    per_chunk = rows // BLK
    blocks = chunks * per_chunk

    lane = lax.broadcasted_iota(jnp.int32, (TAIL, 2 * HEAD), 1)
    for c in range(chunks):
        listed = x_refs[c][rows:, :].astype(jnp.float32).astype(jnp.int32)
        part = lax.rem(lax.axis_index("col") - lax.div(listed, per_chunk) + parts, parts)
        slot = part * per_chunk + lax.rem(listed, per_chunk)
        wide[c * TAIL : (c + 1) * TAIL, :] = jnp.where(lane < MAXNB, slot, listed)
    table_copy = pltpu.make_async_copy(wide, table, table_sem)
    table_copy.start()

    copies = []
    if first:
        for c in range(parts):
            copies.append(
                pltpu.make_async_copy(
                    kv_refs[c], kv_all.at[pl.ds(c * rows, rows), :], sem.at[c]
                )
            )
    for copy in copies:
        copy.start()
    for s in range(STREAMS):
        accs[s][...] = jnp.zeros_like(accs[s])
        outs[s][...] = jnp.zeros_like(outs[s])
        stats[s][0] = jnp.full(stats[s].shape[1:], NEG_FILL, jnp.float32)
        stats[s][1] = jnp.zeros(stats[s].shape[1:], jnp.float32)
        stats[s][2] = jnp.zeros(stats[s].shape[1:], jnp.float32)

    is_left = lax.broadcasted_iota(jnp.int32, (BLK, 2 * HEAD), 1) < HEAD
    zeros = jnp.zeros((HEAD, BLK), jnp.bfloat16)
    for b in range(blocks):
        at = (b % per_chunk) * BLK
        x = x_refs[b // per_chunk][at : at + BLK, :]
        both[b, :BLK, :] = jnp.where(is_left, x, jnp.zeros_like(x))
        both[b, BLK:, :] = jnp.where(is_left, jnp.zeros_like(x), x)
        x_t = x.T
        both_t[b, :HEAD, :BLK] = x_t[:HEAD]
        both_t[b, :HEAD, BLK:] = zeros
        both_t[b, HEAD:, :BLK] = zeros
        both_t[b, HEAD:, BLK:] = x_t[HEAD:]
    if first:
        for c in range(parts):
            for b in range(per_chunk):
                at = c * rows + b * BLK
                kv_t[:, at : at + BLK] = kv_refs[c][b * BLK : (b + 1) * BLK, :].T
    for copy in copies:
        copy.wait()
    table_copy.wait()

    def line(qb):
        return lax.div(qb, per_chunk) * TAIL + lax.rem(qb, per_chunk)

    def add_items(qb, count):
        groups = (table[line(qb), MAXNB] + GROUP - 1) // GROUP

        def add_item(g, _):
            items[0, count + g] = qb
            items[1, count + g] = g * GROUP
            return 0

        lax.fori_loop(0, groups, add_item, 0)
        return count + groups

    count = lax.fori_loop(0, blocks, add_items, 0)
    steps = (count + STREAMS - 1) // STREAMS
    for s in range(STREAMS - 1):
        items[0, count + s] = 0
        items[1, count + s] = MAXNB

    def item(at):
        qb, base = items[0, at], items[1, at]
        slots = [
            pl.multiple_of(table[line(qb), jnp.minimum(base + u, MAXNB - 1)] * BLK, BLK)
            for u in range(GROUP)
        ]
        return qb, base, slots

    def score_step(i, _):
        for s in range(STREAMS):
            at = s * steps + i
            qb, base, slots = item(at)
            live = table[line(qb), MAXNB]
            kv = jnp.concatenate([kv_all[pl.ds(k, BLK), :] for k in slots], axis=0)
            both_scores = jnp.dot(kv, both_t[qb], preferred_element_type=jnp.float32)
            scores = [
                both_scores[u * BLK : (u + 1) * BLK, :BLK] * to_log2
                + jnp.where(base + u < live, 0.0, NEG_FILL)
                for u in range(GROUP)
            ]
            top = functools.reduce(jnp.maximum, [fold(v, jnp.max) for v in scores])
            top = jnp.max(top, axis=0, keepdims=True)
            total = jnp.zeros((8, BLK), jnp.float32)
            dot = jnp.zeros((8, BLK), jnp.float32)
            for u in range(GROUP):
                part = slice(u * BLK, (u + 1) * BLK)
                e = jnp.exp2(scores[u] - top)
                dw = both_scores[part, BLK:]
                tiles[at, part, :BLK] = e
                tiles[at, part, BLK:] = dw
                total = total + fold(e, jnp.sum)
                dot = dot + fold(e * dw, jnp.sum)
            total = jnp.sum(total, axis=0, keepdims=True)
            dot = jnp.sum(dot, axis=0, keepdims=True)
            tops[pl.ds(at, 1), :] = top
            row = pl.ds(qb, 1)
            old = stats[s][0, row, :]
            new = jnp.maximum(old, top)
            old_part, new_part = jnp.exp2(old - new), jnp.exp2(top - new)
            stats[s][0, row, :] = new
            stats[s][1, row, :] = stats[s][1, row, :] * old_part + total * new_part
            stats[s][2, row, :] = stats[s][2, row, :] * old_part + dot * new_part
        return 0

    lax.fori_loop(0, steps, score_step, 0)

    top = functools.reduce(jnp.maximum, [st[0] for st in stats])
    total = functools.reduce(jnp.add, [st[1] * jnp.exp2(st[0] - top) for st in stats])
    dot = functools.reduce(jnp.add, [st[2] * jnp.exp2(st[0] - top) for st in stats])
    stat[0] = top
    stat[1] = 1.0 / total
    stat[2] = dot / total

    def grad_step(i, _):
        for s in range(STREAMS):
            at = s * steps + i
            qb, base, slots = item(at)
            row = pl.ds(qb, 1)
            factor = stat[1, row, :] * jnp.exp2(tops[pl.ds(at, 1), :] - stat[0, row, :])
            delta = stat[2, row, :]
            w, ds = [], []
            for u in range(GROUP):
                part = slice(u * BLK, (u + 1) * BLK)
                weights = tiles[at, part, :BLK] * factor
                ds.append((weights * (tiles[at, part, BLK:] - delta)).astype(jnp.bfloat16))
                w.append(weights.astype(jnp.bfloat16))
            pair = jnp.concatenate(
                [jnp.concatenate(ds, axis=0), jnp.concatenate(w, axis=0)], axis=1
            )
            grads = jnp.dot(pair, both[qb], preferred_element_type=jnp.float32)
            for u in range(GROUP):
                accs[s][pl.ds(slots[u], BLK), :] += grads[u * BLK : (u + 1) * BLK]
            t = jnp.concatenate([kv_t[:, pl.ds(k, BLK)] for k in slots], axis=1)
            sums = jnp.dot(t, pair, preferred_element_type=jnp.float32)
            outs[s][qb, :HEAD, :] += sums[HEAD:, BLK:]
            outs[s][qb, HEAD:, :] += sums[:HEAD, :BLK]
        return 0

    lax.fori_loop(0, steps, grad_step, 0)

    is_out = lax.broadcasted_iota(jnp.int32, (2 * HEAD, BLK), 0) < HEAD
    for b in range(blocks):
        out = functools.reduce(jnp.add, [r[b] for r in outs])
        out = jnp.where(is_out, out, out * scale)
        at = (b % per_chunk) * BLK
        og_refs[b // per_chunk][at : at + BLK, :] = out.T.astype(jnp.bfloat16)
    for b in range(parts * per_chunk):
        part = slice(b * BLK, (b + 1) * BLK)
        acc = functools.reduce(jnp.add, [r[part, :] for r in accs])
        if not first:
            acc = acc + acc_in[part, :]
        if last:
            at = (b % per_chunk) * BLK
            acc = jnp.where(is_left, acc * scale, acc)
            gkv_refs[b // per_chunk][at : at + BLK, :] = acc.astype(jnp.bfloat16)
        else:
            acc_out[part, :] = acc


def in_vmem(x):
    return pltpu.with_memory_space_constraint(x, pltpu.VMEM)


def head_per_device(queries, keys, values, cotangent, block_lists, block_counts):
    chunks = 4
    rows = queries.shape[0]
    chunk = pltpu.VMEM((rows, 2 * HEAD), jnp.bfloat16)
    tailed = pltpu.VMEM((rows + TAIL, 2 * HEAD), jnp.bfloat16)
    packed = pl.pallas_call(
        pack_body,
        out_shape=[tailed] * chunks + [chunk] * chunks,
        in_specs=[SMEM] * 2 + [VMEM] * 4,
        out_specs=[VMEM] * (2 * chunks),
        name="pack",
    )(block_lists, block_counts, queries, cotangent, keys, values)

    def q_perm(step):
        return [
            (r * chunks + c, c * chunks + (r + step) % chunks)
            for r in range(chunks)
            for c in range(chunks)
        ]

    def k_perm(step):
        return [(c, (c + step) % chunks) for c in range(chunks)]

    def swap(perm):
        return [(b, a) for a, b in perm]

    axes = ("row", "col")
    kv = [packed[chunks]] + [
        lax.ppermute(packed[chunks + s], "col", k_perm(s)) for s in range(1, chunks)
    ]
    xs = [lax.ppermute(packed[s], axes, q_perm(s)) for s in range(chunks)]

    def attend(xs, carried, first, last):
        count = len(xs)
        blocks = count * rows // BLK
        most = blocks * MAXNB // GROUP + STREAMS
        keys_all = pltpu.VMEM((chunks * rows, 2 * HEAD), jnp.bfloat16)
        keys_t = pltpu.VMEM((2 * HEAD, chunks * rows), jnp.bfloat16)
        sums = pltpu.VMEM((chunks * rows, 2 * HEAD), jnp.float32)
        out_shape = [chunk] * count + ([chunk] * chunks if last else [sums])
        if first:
            out_shape += [keys_all, keys_t]
        return pl.pallas_call(
            functools.partial(attend_body, count, chunks, first, last),
            out_shape=out_shape,
            in_specs=[VMEM] * (count + len(carried)),
            out_specs=[VMEM] * len(out_shape),
            scratch_shapes=[
                pltpu.VMEM((count * TAIL, 2 * HEAD), jnp.int32),
                pltpu.SMEM((count * TAIL, 2 * HEAD), jnp.int32),
                pltpu.SMEM((2, most), jnp.int32),
                pltpu.VMEM((blocks, 2 * BLK, 2 * HEAD), jnp.bfloat16),
                pltpu.VMEM((blocks, 2 * HEAD, 2 * BLK), jnp.bfloat16),
                pltpu.VMEM((3, blocks, BLK), jnp.float32),
                pltpu.VMEM((most, GROUP * BLK, 2 * BLK), jnp.float32),
                pltpu.VMEM((most, BLK), jnp.float32),
                pltpu.SemaphoreType.DMA((chunks,)),
                pltpu.SemaphoreType.DMA,
            ]
            + [sums] * STREAMS
            + [pltpu.VMEM((blocks, 2 * HEAD, BLK), jnp.float32)] * STREAMS
            + [pltpu.VMEM((3, blocks, BLK), jnp.float32)] * STREAMS,
            compiler_params=pltpu.CompilerParams(vmem_limit_bytes=VMEM_LIMIT),
            name="attend",
        )(*[in_vmem(a) for a in (*xs, *carried)])

    carried = kv
    ogs = []
    for size in BATCHES:
        batch = xs[len(ogs) : len(ogs) + size]
        first, last = not ogs, len(ogs) + size == chunks
        results = attend(batch, carried, first, last)
        ogs += [
            lax.ppermute(results[s], axes, swap(q_perm(len(ogs) + s))) for s in range(size)
        ]
        rest = results[size:]
        if last:
            gkv = rest[:chunks]
        elif first:
            keys_all, keys_t = rest[1:]
        carried = [keys_all, keys_t, rest[0]] if not last else None
    gkv = [gkv[0]] + [lax.ppermute(gkv[s], "col", swap(k_perm(s))) for s in range(1, chunks)]

    whole = jax.ShapeDtypeStruct(queries.shape, jnp.bfloat16)

    def unpack(axis, parts):
        return pl.pallas_call(
            functools.partial(unpack_body, axis),
            out_shape=[whole, whole],
            in_specs=[VMEM] * chunks,
            out_specs=[VMEM, VMEM],
            name="unpack",
        )(*[in_vmem(p) for p in parts])

    attended, grad_queries = unpack("row", ogs)
    grad_keys, grad_values = unpack("col", gkv)
    return attended, grad_queries, grad_keys, grad_values


def tile_scores(query_tile, key_tile, score_scale):
    query_heads = query_tile.reshape(query_tile.shape[0], HEADS, -1)
    key_heads = key_tile.reshape(key_tile.shape[0], HEADS, -1)
    return (
        jnp.einsum("qhd,khd->hqk", query_heads, key_heads, preferred_element_type=jnp.float32)
        * score_scale
    )


def on_device(queries, keys, values, cotangent, block_lists, block_counts):
    score_scale = 1.0 / math.sqrt(HEAD)
    q_full = lax.all_gather(queries, "col", axis=1, tiled=True)
    k_full, v_full = (
        lax.all_gather(keys, "row", axis=1, tiled=True),
        lax.all_gather(values, "row", axis=1, tiled=True),
    )
    q_rows = q_full.shape[0]
    k_rows = k_full.shape[0]
    q_blocks = q_rows // BLK
    k_blocks = k_rows // BLK
    group_size = min(4, q_blocks)
    span_rows = group_size * BLK
    supers = q_blocks // group_size
    tile_count = supers * k_blocks
    first_key = lax.axis_index("col") * k_blocks
    wanted = first_key + jnp.arange(k_blocks, dtype=jnp.int32)
    live_slots = jnp.arange(MAXNB, dtype=jnp.int32)[None, :] < block_counts[:, None]
    block_hit = jnp.any(
        (block_lists[:, :, None] == wanted[None, None, :]) & live_slots[:, :, None], axis=1
    )
    block_hit = block_hit.reshape(supers, group_size, k_blocks).transpose(0, 2, 1)
    row_mask = jnp.repeat(block_hit, BLK, axis=2)
    tile_any = jnp.any(block_hit, axis=2)

    def tile_parts(step):
        super_at = step // k_blocks
        key_at = step % k_blocks
        query_tile = lax.dynamic_slice_in_dim(q_full, super_at * span_rows, span_rows, 0)
        key_tile = lax.dynamic_slice_in_dim(k_full, key_at * BLK, BLK, 0)
        value_tile = lax.dynamic_slice_in_dim(v_full, key_at * BLK, BLK, 0)
        keep_mask = row_mask[super_at, key_at][None, :, None]
        return (super_at, key_at, query_tile, key_tile, value_tile, keep_mask)

    def unchanged(carry):
        return carry

    def stats_step(step, carry):
        super_at, key_at, query_tile, key_tile, value_tile, keep_mask = tile_parts(step)

        def stats_work(state):
            row_top, row_total = state
            scores = jnp.where(keep_mask, tile_scores(query_tile, key_tile, score_scale), NEG_FILL)
            old_top = lax.dynamic_slice_in_dim(row_top, super_at * span_rows, span_rows, 1)
            old_total = lax.dynamic_slice_in_dim(row_total, super_at * span_rows, span_rows, 1)
            new_top = jnp.maximum(old_top, jnp.max(scores, axis=2))
            exp_terms = jnp.where(keep_mask, jnp.exp(scores - new_top[:, :, None]), 0.0)
            fresh = old_total * jnp.exp(old_top - new_top) + jnp.sum(exp_terms, axis=2)
            return (
                lax.dynamic_update_slice_in_dim(row_top, new_top, super_at * span_rows, 1),
                lax.dynamic_update_slice_in_dim(row_total, fresh, super_at * span_rows, 1),
            )

        return lax.cond(tile_any[super_at, key_at], stats_work, unchanged, carry)

    start_top = jnp.full((HEADS, q_rows), NEG_FILL, jnp.float32)
    start_total = jnp.zeros((HEADS, q_rows), jnp.float32)
    local_top, local_total = lax.fori_loop(0, tile_count, stats_step, (start_top, start_total))
    row_top = lax.pmax(local_top.astype(jnp.bfloat16), "col").astype(local_top.dtype)
    row_total = lax.psum(local_total * jnp.exp(local_top - row_top), "col")

    def tile_weights(scores, super_at, keep_mask):
        top_rows = lax.dynamic_slice_in_dim(row_top, super_at * span_rows, span_rows, 1)
        total_rows = lax.dynamic_slice_in_dim(row_total, super_at * span_rows, span_rows, 1)
        ratio = jnp.exp(scores - top_rows[:, :, None]) / total_rows[:, :, None]
        return jnp.where(keep_mask, ratio, 0.0).astype(jnp.bfloat16)

    def output_step(step, carry):
        super_at, key_at, query_tile, key_tile, value_tile, keep_mask = tile_parts(step)

        def output_work(out_rows):
            scores = jnp.where(keep_mask, tile_scores(query_tile, key_tile, score_scale), NEG_FILL)
            weights = tile_weights(scores, super_at, keep_mask)
            value_heads = value_tile.reshape(BLK, HEADS, -1)
            part = jnp.einsum(
                "hqk,khd->qhd", weights, value_heads, preferred_element_type=jnp.float32
            ).reshape(span_rows, -1)
            current = lax.dynamic_slice_in_dim(out_rows, super_at * span_rows, span_rows, 0)
            return lax.dynamic_update_slice_in_dim(
                out_rows, current + part, super_at * span_rows, 0
            )

        return lax.cond(tile_any[super_at, key_at], output_work, unchanged, carry)

    partial_out = lax.fori_loop(0, tile_count, output_step, jnp.zeros((q_rows, D), jnp.float32))
    out_share = lax.psum_scatter(partial_out, "col", scatter_dimension=1, tiled=True).astype(
        jnp.bfloat16
    )
    grad_full, out_full = (
        lax.all_gather(cotangent, "col", axis=1, tiled=True),
        lax.all_gather(out_share, "col", axis=1, tiled=True),
    )
    delta = jnp.einsum(
        "qhd,qhd->hq",
        grad_full.reshape(q_rows, HEADS, -1),
        out_full.reshape(q_rows, HEADS, -1),
        preferred_element_type=jnp.float32,
    )

    def grad_step(step, carry):
        super_at, key_at, query_tile, key_tile, value_tile, keep_mask = tile_parts(step)

        def grad_work(state):
            query_accum, key_accum, value_accum = state
            scores = jnp.where(keep_mask, tile_scores(query_tile, key_tile, score_scale), NEG_FILL)
            weights = tile_weights(scores, super_at, keep_mask)
            grad_tile = lax.dynamic_slice_in_dim(
                grad_full, super_at * span_rows, span_rows, 0
            ).reshape(span_rows, HEADS, -1)
            value_heads = value_tile.reshape(BLK, HEADS, -1)
            key_heads = key_tile.reshape(BLK, HEADS, -1)
            query_heads = query_tile.reshape(span_rows, HEADS, -1)
            dweights = jnp.einsum(
                "qhd,khd->hqk", grad_tile, value_heads, preferred_element_type=jnp.float32
            )
            delta_rows = lax.dynamic_slice_in_dim(delta, super_at * span_rows, span_rows, 1)
            dscores = (weights.astype(jnp.float32) * (dweights - delta_rows[:, :, None])).astype(
                jnp.bfloat16
            )
            query_part = score_scale * jnp.einsum(
                "hqk,khd->qhd", dscores, key_heads, preferred_element_type=jnp.float32
            )
            key_part = score_scale * jnp.einsum(
                "hqk,qhd->khd", dscores, query_heads, preferred_element_type=jnp.float32
            )
            value_part = jnp.einsum(
                "hqk,qhd->khd", weights, grad_tile, preferred_element_type=jnp.float32
            )
            query_now = lax.dynamic_slice_in_dim(query_accum, super_at * span_rows, span_rows, 0)
            key_now = lax.dynamic_slice_in_dim(key_accum, key_at * BLK, BLK, 0)
            value_now = lax.dynamic_slice_in_dim(value_accum, key_at * BLK, BLK, 0)
            query_accum = lax.dynamic_update_slice_in_dim(
                query_accum, query_now + query_part.reshape(span_rows, -1), super_at * span_rows, 0
            )
            key_accum = lax.dynamic_update_slice_in_dim(
                key_accum, key_now + key_part.reshape(BLK, -1), key_at * BLK, 0
            )
            value_accum = lax.dynamic_update_slice_in_dim(
                value_accum, value_now + value_part.reshape(BLK, -1), key_at * BLK, 0
            )
            return (query_accum, key_accum, value_accum)

        return lax.cond(tile_any[super_at, key_at], grad_work, unchanged, carry)

    start_grads = (
        jnp.zeros((q_rows, D), jnp.float32),
        jnp.zeros((k_rows, D), jnp.float32),
        jnp.zeros((k_rows, D), jnp.float32),
    )
    query_parts, key_parts, value_parts = lax.fori_loop(0, tile_count, grad_step, start_grads)
    grad_queries = lax.psum_scatter(query_parts, "col", scatter_dimension=1, tiled=True).astype(
        jnp.bfloat16
    )
    grad_keys, grad_values = (
        lax.psum_scatter(key_parts, "row", scatter_dimension=1, tiled=True),
        lax.psum_scatter(value_parts, "row", scatter_dimension=1, tiled=True),
    )
    return (
        out_share,
        grad_queries,
        grad_keys.astype(jnp.bfloat16),
        grad_values.astype(jnp.bfloat16),
    )


def solution(mesh):
    rows, cols = mesh.shape["row"], mesh.shape["col"]
    one_head = rows == 4 and cols == 4
    return jax.shard_map(
        head_per_device if one_head else on_device,
        mesh=mesh,
        in_specs=(
            P(("groups", "row"), "col"),
            P(("groups", "col"), "row"),
            P(("groups", "col"), "row"),
            P(("groups", "row"), "col"),
            P(("groups", "row"), None),
            P(("groups", "row")),
        ),
        out_specs=(
            P(("groups", "row"), "col"),
            P(("groups", "row"), "col"),
            P(("groups", "col"), "row"),
            P(("groups", "col"), "row"),
        ),
        check_vma=False,
    )
```

```python
import functools
import math

import jax
import jax.numpy as jnp
from jax import lax
from jax.experimental import pallas as pl
from jax.experimental.pallas import tpu as pltpu
from jax.sharding import PartitionSpec as P

D = 1024
HEADS = 16
HEAD = 64
BLK = 128
MAXNB = 16


NEG_FILL = -1e30
GROUP = 2
STREAMS = 8
TAIL = 16
BATCHES = (1, 2, 1)
HOPS = (2, 3)
VMEM_LIMIT = 40 * 1024 * 1024
VMEM = pl.BlockSpec(memory_space=pltpu.VMEM)
SMEM = pl.BlockSpec(memory_space=pltpu.SMEM)


def pack_body(lists, counts, q_ref, g_ref, k_ref, v_ref, *outs):
    chunks = q_ref.shape[1] // HEAD
    rows = q_ref.shape[0]

    def pack(left_ref, right_ref, out_refs, at):
        for step in range(chunks):
            head = (at + step) % chunks
            lanes = slice(head * HEAD, (head + 1) * HEAD)
            out_refs[step][:rows, :] = jnp.concatenate(
                [left_ref[:, lanes], right_ref[:, lanes]], axis=1
            )

    for at in range(chunks):

        @pl.when(lax.axis_index("col") == at)
        def _():
            pack(k_ref, v_ref, outs[chunks:], at)

        @pl.when(lax.axis_index("row") == at)
        def _():
            pack(q_ref, g_ref, outs[:chunks], at)

    row = lax.broadcasted_iota(jnp.int32, (TAIL, 2 * HEAD), 0)
    lane = lax.broadcasted_iota(jnp.int32, (TAIL, 2 * HEAD), 1)
    table = jnp.zeros((TAIL, 2 * HEAD), jnp.int32)
    for qb in range(rows // BLK):
        line = jnp.where(lane == MAXNB, counts[qb], 0)
        for at in range(MAXNB):
            line = jnp.where(lane == at, lists[qb, at], line)
        table = jnp.where(row == qb, line, table)
    table = table.astype(jnp.float32).astype(jnp.bfloat16)
    for out_ref in outs[:chunks]:
        out_ref[rows:, :] = table


def unpack_body(axis, *refs):
    left_ref, right_ref = refs[-2:]
    chunks = len(refs) - 2
    for at in range(chunks):

        @pl.when(lax.axis_index(axis) == at)
        def _():
            parts = [refs[(head - at) % chunks][...] for head in range(chunks)]
            left_ref[...] = jnp.concatenate([p[:, :HEAD] for p in parts], axis=1)
            right_ref[...] = jnp.concatenate([p[:, HEAD:] for p in parts], axis=1)


def fold(x, op):
    return op(x.reshape(x.shape[0] // 8, 8, x.shape[1]), axis=0)


def attend_body(chunks, parts, first, last, *refs):
    def take(count):
        nonlocal refs
        head, refs = refs[:count], refs[count:]
        return head

    x_refs = take(chunks)
    if first:
        kv_refs = take(parts)
    else:
        kv_all, kv_t, acc_in = take(3)
    og_refs = take(chunks)
    gkv_refs = take(parts) if last else ()
    acc_out = () if last else take(1)
    if first:
        kv_all, kv_t = take(2)
    wide, table, items, both, both_t, stat, tiles, tops, sem, table_sem = take(10)
    (outs,) = take(1)
    stats = take(STREAMS)
    acc = take(1)[0] if last else acc_out[0]
    scale = 1.0 / math.sqrt(HEAD)
    to_log2 = scale * math.log2(math.e)
    rows = kv_all.shape[0] // parts
    per_chunk = rows // BLK
    blocks = chunks * per_chunk

    lane = lax.broadcasted_iota(jnp.int32, (TAIL, 2 * HEAD), 1)
    for c in range(chunks):
        listed = x_refs[c][rows:, :].astype(jnp.float32).astype(jnp.int32)
        part = lax.rem(lax.axis_index("col") - lax.div(listed, per_chunk) + parts, parts)
        slot = part * per_chunk + lax.rem(listed, per_chunk)
        wide[c * TAIL : (c + 1) * TAIL, :] = jnp.where(lane < MAXNB, slot, listed)
    table_copy = pltpu.make_async_copy(wide, table, table_sem)
    table_copy.start()

    copies = []
    if first:
        for c in range(parts):
            copies.append(
                pltpu.make_async_copy(
                    kv_refs[c], kv_all.at[pl.ds(c * rows, rows), :], sem.at[c]
                )
            )
    for copy in copies:
        copy.start()
    if first:
        acc[...] = jnp.zeros_like(acc)
    else:
        acc[...] = acc_in[...]
    outs[...] = jnp.zeros_like(outs)
    for s in range(STREAMS):
        stats[s][0] = jnp.full(stats[s].shape[1:], NEG_FILL, jnp.float32)
        stats[s][1] = jnp.zeros(stats[s].shape[1:], jnp.float32)
        stats[s][2] = jnp.zeros(stats[s].shape[1:], jnp.float32)

    is_left = lax.broadcasted_iota(jnp.int32, (BLK, 2 * HEAD), 1) < HEAD
    zeros = jnp.zeros((HEAD, BLK), jnp.bfloat16)
    for b in range(blocks):
        at = (b % per_chunk) * BLK
        x = x_refs[b // per_chunk][at : at + BLK, :]
        both[b, :BLK, :] = jnp.where(is_left, x, jnp.zeros_like(x))
        both[b, BLK:, :] = jnp.where(is_left, jnp.zeros_like(x), x)
        x_t = x.T
        both_t[b, :HEAD, :BLK] = x_t[:HEAD]
        both_t[b, :HEAD, BLK:] = zeros
        both_t[b, HEAD:, :BLK] = zeros
        both_t[b, HEAD:, BLK:] = x_t[HEAD:]
    if first:
        for c in range(parts):
            for b in range(per_chunk):
                at = c * rows + b * BLK
                kv_t[:, at : at + BLK] = kv_refs[c][b * BLK : (b + 1) * BLK, :].T
    for copy in copies:
        copy.wait()
    table_copy.wait()

    def line(qb):
        return lax.div(qb, per_chunk) * TAIL + lax.rem(qb, per_chunk)

    def add_items(qb, count):
        groups = (table[line(qb), MAXNB] + GROUP - 1) // GROUP

        def add_item(g, _):
            items[0, count + g] = qb
            items[1, count + g] = g * GROUP
            return 0

        lax.fori_loop(0, groups, add_item, 0)
        return count + groups

    count = lax.fori_loop(0, blocks, add_items, 0)
    steps = (count + STREAMS - 1) // STREAMS
    for s in range(STREAMS - 1):
        items[0, count + s] = 0
        items[1, count + s] = MAXNB

    def item(at):
        qb, base = items[0, at], items[1, at]
        slots = [
            pl.multiple_of(table[line(qb), jnp.minimum(base + u, MAXNB - 1)] * BLK, BLK)
            for u in range(GROUP)
        ]
        return qb, base, slots

    def score_step(i, _):
        for s in range(STREAMS):
            at = s * steps + i
            qb, base, slots = item(at)
            live = table[line(qb), MAXNB]
            kv = jnp.concatenate([kv_all[pl.ds(k, BLK), :] for k in slots], axis=0)
            both_scores = jnp.dot(kv, both_t[qb], preferred_element_type=jnp.float32)
            scores = [
                both_scores[u * BLK : (u + 1) * BLK, :BLK] * to_log2
                + jnp.where(base + u < live, 0.0, NEG_FILL)
                for u in range(GROUP)
            ]
            top = functools.reduce(jnp.maximum, [fold(v, jnp.max) for v in scores])
            top = jnp.max(top, axis=0, keepdims=True)
            total = jnp.zeros((8, BLK), jnp.float32)
            dot = jnp.zeros((8, BLK), jnp.float32)
            for u in range(GROUP):
                part = slice(u * BLK, (u + 1) * BLK)
                e = jnp.exp2(scores[u] - top)
                dw = both_scores[part, BLK:]
                tiles[at, part, :BLK] = e
                tiles[at, part, BLK:] = dw
                total = total + fold(e, jnp.sum)
                dot = dot + fold(e * dw, jnp.sum)
            total = jnp.sum(total, axis=0, keepdims=True)
            dot = jnp.sum(dot, axis=0, keepdims=True)
            tops[pl.ds(at, 1), :] = top
            row = pl.ds(qb, 1)
            old = stats[s][0, row, :]
            new = jnp.maximum(old, top)
            old_part, new_part = jnp.exp2(old - new), jnp.exp2(top - new)
            stats[s][0, row, :] = new
            stats[s][1, row, :] = stats[s][1, row, :] * old_part + total * new_part
            stats[s][2, row, :] = stats[s][2, row, :] * old_part + dot * new_part
        return 0

    lax.fori_loop(0, steps, score_step, 0)

    top = functools.reduce(jnp.maximum, [st[0] for st in stats])
    total = functools.reduce(jnp.add, [st[1] * jnp.exp2(st[0] - top) for st in stats])
    dot = functools.reduce(jnp.add, [st[2] * jnp.exp2(st[0] - top) for st in stats])
    stat[0] = top
    stat[1] = 1.0 / total
    stat[2] = dot / total

    def grad_step(i, _):
        for s in range(STREAMS):
            at = s * steps + i
            qb, base, slots = item(at)
            row = pl.ds(qb, 1)
            factor = stat[1, row, :] * jnp.exp2(tops[pl.ds(at, 1), :] - stat[0, row, :])
            delta = stat[2, row, :]
            w, ds = [], []
            for u in range(GROUP):
                part = slice(u * BLK, (u + 1) * BLK)
                weights = tiles[at, part, :BLK] * factor
                ds.append((weights * (tiles[at, part, BLK:] - delta)).astype(jnp.bfloat16))
                w.append(weights.astype(jnp.bfloat16))
            pair = jnp.concatenate(
                [jnp.concatenate(ds, axis=0), jnp.concatenate(w, axis=0)], axis=1
            )
            grads = jnp.dot(pair, both[qb], preferred_element_type=jnp.float32)
            for u in range(GROUP):
                acc[pl.ds(slots[u], BLK), :] += grads[u * BLK : (u + 1) * BLK]
            t = jnp.concatenate([kv_t[:, pl.ds(k, BLK)] for k in slots], axis=1)
            sums = jnp.dot(t, pair, preferred_element_type=jnp.float32)
            outs[qb, :HEAD, :] += sums[HEAD:, BLK:]
            outs[qb, HEAD:, :] += sums[:HEAD, :BLK]
        return 0

    lax.fori_loop(0, steps, grad_step, 0)

    is_out = lax.broadcasted_iota(jnp.int32, (2 * HEAD, BLK), 0) < HEAD
    for b in range(blocks):
        out = outs[b]
        out = jnp.where(is_out, out, out * scale)
        at = (b % per_chunk) * BLK
        og_refs[b // per_chunk][at : at + BLK, :] = out.T.astype(jnp.bfloat16)
    if last:
        for b in range(parts * per_chunk):
            total = acc[b * BLK : (b + 1) * BLK, :]
            at = (b % per_chunk) * BLK
            gkv_refs[b // per_chunk][at : at + BLK, :] = jnp.where(
                is_left, total * scale, total
            ).astype(jnp.bfloat16)


def in_vmem(x):
    return pltpu.with_memory_space_constraint(x, pltpu.VMEM)


def head_per_device(queries, keys, values, cotangent, block_lists, block_counts):
    chunks = 4
    rows = queries.shape[0]
    chunk = pltpu.VMEM((rows, 2 * HEAD), jnp.bfloat16)
    tailed = pltpu.VMEM((rows + TAIL, 2 * HEAD), jnp.bfloat16)
    packed = pl.pallas_call(
        pack_body,
        out_shape=[tailed] * chunks + [chunk] * chunks,
        in_specs=[SMEM] * 2 + [VMEM] * 4,
        out_specs=[VMEM] * (2 * chunks),
        name="pack",
    )(block_lists, block_counts, queries, cotangent, keys, values)

    def q_perm(step):
        return [
            (r * chunks + c, c * chunks + (r + step) % chunks)
            for r in range(chunks)
            for c in range(chunks)
        ]

    def k_perm(step):
        return [(c, (c + step) % chunks) for c in range(chunks)]

    def swap(perm):
        return [(b, a) for a, b in perm]

    axes = ("row", "col")
    kv = [packed[chunks]] + [
        lax.ppermute(packed[chunks + s], "col", k_perm(s)) for s in range(1, chunks)
    ]
    hop = {s: lax.ppermute(packed[s], "col", [(c, c ^ 2) for c in range(chunks)]) for s in HOPS}
    xs = [
        lax.ppermute(
            hop.get(s, packed[s]), axes, [(a ^ 2, b) if s in hop else (a, b) for a, b in q_perm(s)]
        )
        for s in range(chunks)
    ]

    def attend(xs, carried, first, last):
        count = len(xs)
        blocks = count * rows // BLK
        most = blocks * MAXNB // GROUP + STREAMS
        keys_all = pltpu.VMEM((chunks * rows, 2 * HEAD), jnp.bfloat16)
        keys_t = pltpu.VMEM((2 * HEAD, chunks * rows), jnp.bfloat16)
        sums = pltpu.VMEM((chunks * rows, 2 * HEAD), jnp.float32)
        out_shape = [chunk] * count + ([chunk] * chunks if last else [sums])
        if first:
            out_shape += [keys_all, keys_t]
        return pl.pallas_call(
            functools.partial(attend_body, count, chunks, first, last),
            out_shape=out_shape,
            in_specs=[VMEM] * (count + len(carried)),
            out_specs=[VMEM] * len(out_shape),
            scratch_shapes=[
                pltpu.VMEM((count * TAIL, 2 * HEAD), jnp.int32),
                pltpu.SMEM((count * TAIL, 2 * HEAD), jnp.int32),
                pltpu.SMEM((2, most), jnp.int32),
                pltpu.VMEM((blocks, 2 * BLK, 2 * HEAD), jnp.bfloat16),
                pltpu.VMEM((blocks, 2 * HEAD, 2 * BLK), jnp.bfloat16),
                pltpu.VMEM((3, blocks, BLK), jnp.float32),
                pltpu.VMEM((most, GROUP * BLK, 2 * BLK), jnp.float32),
                pltpu.VMEM((most, BLK), jnp.float32),
                pltpu.SemaphoreType.DMA((chunks,)),
                pltpu.SemaphoreType.DMA,
            ]
            + [pltpu.VMEM((blocks, 2 * HEAD, BLK), jnp.float32)]
            + [pltpu.VMEM((3, blocks, BLK), jnp.float32)] * STREAMS
            + ([sums] if last else []),
            compiler_params=pltpu.CompilerParams(vmem_limit_bytes=VMEM_LIMIT),
            name="attend",
        )(*[in_vmem(a) for a in (*xs, *carried)])

    carried = kv
    ogs = []
    for size in BATCHES:
        batch = xs[len(ogs) : len(ogs) + size]
        first, last = not ogs, len(ogs) + size == chunks
        results = attend(batch, carried, first, last)
        ogs += [
            lax.ppermute(results[s], axes, swap(q_perm(len(ogs) + s))) for s in range(size)
        ]
        rest = results[size:]
        if last:
            gkv = rest[:chunks]
        elif first:
            keys_all, keys_t = rest[1:]
        carried = [keys_all, keys_t, rest[0]] if not last else None
    gkv = [gkv[0]] + [lax.ppermute(gkv[s], "col", swap(k_perm(s))) for s in range(1, chunks)]

    whole = jax.ShapeDtypeStruct(queries.shape, jnp.bfloat16)

    def unpack(axis, parts):
        return pl.pallas_call(
            functools.partial(unpack_body, axis),
            out_shape=[whole, whole],
            in_specs=[VMEM] * chunks,
            out_specs=[VMEM, VMEM],
            name="unpack",
        )(*[in_vmem(p) for p in parts])

    attended, grad_queries = unpack("row", ogs)
    grad_keys, grad_values = unpack("col", gkv)
    return attended, grad_queries, grad_keys, grad_values


def tile_scores(query_tile, key_tile, score_scale):
    query_heads = query_tile.reshape(query_tile.shape[0], HEADS, -1)
    key_heads = key_tile.reshape(key_tile.shape[0], HEADS, -1)
    return (
        jnp.einsum("qhd,khd->hqk", query_heads, key_heads, preferred_element_type=jnp.float32)
        * score_scale
    )


def on_device(queries, keys, values, cotangent, block_lists, block_counts):
    score_scale = 1.0 / math.sqrt(HEAD)
    q_full = lax.all_gather(queries, "col", axis=1, tiled=True)
    k_full, v_full = (
        lax.all_gather(keys, "row", axis=1, tiled=True),
        lax.all_gather(values, "row", axis=1, tiled=True),
    )
    q_rows = q_full.shape[0]
    k_rows = k_full.shape[0]
    q_blocks = q_rows // BLK
    k_blocks = k_rows // BLK
    group_size = min(4, q_blocks)
    span_rows = group_size * BLK
    supers = q_blocks // group_size
    tile_count = supers * k_blocks
    first_key = lax.axis_index("col") * k_blocks
    wanted = first_key + jnp.arange(k_blocks, dtype=jnp.int32)
    live_slots = jnp.arange(MAXNB, dtype=jnp.int32)[None, :] < block_counts[:, None]
    block_hit = jnp.any(
        (block_lists[:, :, None] == wanted[None, None, :]) & live_slots[:, :, None], axis=1
    )
    block_hit = block_hit.reshape(supers, group_size, k_blocks).transpose(0, 2, 1)
    row_mask = jnp.repeat(block_hit, BLK, axis=2)
    tile_any = jnp.any(block_hit, axis=2)

    def tile_parts(step):
        super_at = step // k_blocks
        key_at = step % k_blocks
        query_tile = lax.dynamic_slice_in_dim(q_full, super_at * span_rows, span_rows, 0)
        key_tile = lax.dynamic_slice_in_dim(k_full, key_at * BLK, BLK, 0)
        value_tile = lax.dynamic_slice_in_dim(v_full, key_at * BLK, BLK, 0)
        keep_mask = row_mask[super_at, key_at][None, :, None]
        return (super_at, key_at, query_tile, key_tile, value_tile, keep_mask)

    def unchanged(carry):
        return carry

    def stats_step(step, carry):
        super_at, key_at, query_tile, key_tile, value_tile, keep_mask = tile_parts(step)

        def stats_work(state):
            row_top, row_total = state
            scores = jnp.where(keep_mask, tile_scores(query_tile, key_tile, score_scale), NEG_FILL)
            old_top = lax.dynamic_slice_in_dim(row_top, super_at * span_rows, span_rows, 1)
            old_total = lax.dynamic_slice_in_dim(row_total, super_at * span_rows, span_rows, 1)
            new_top = jnp.maximum(old_top, jnp.max(scores, axis=2))
            exp_terms = jnp.where(keep_mask, jnp.exp(scores - new_top[:, :, None]), 0.0)
            fresh = old_total * jnp.exp(old_top - new_top) + jnp.sum(exp_terms, axis=2)
            return (
                lax.dynamic_update_slice_in_dim(row_top, new_top, super_at * span_rows, 1),
                lax.dynamic_update_slice_in_dim(row_total, fresh, super_at * span_rows, 1),
            )

        return lax.cond(tile_any[super_at, key_at], stats_work, unchanged, carry)

    start_top = jnp.full((HEADS, q_rows), NEG_FILL, jnp.float32)
    start_total = jnp.zeros((HEADS, q_rows), jnp.float32)
    local_top, local_total = lax.fori_loop(0, tile_count, stats_step, (start_top, start_total))
    row_top = lax.pmax(local_top.astype(jnp.bfloat16), "col").astype(local_top.dtype)
    row_total = lax.psum(local_total * jnp.exp(local_top - row_top), "col")

    def tile_weights(scores, super_at, keep_mask):
        top_rows = lax.dynamic_slice_in_dim(row_top, super_at * span_rows, span_rows, 1)
        total_rows = lax.dynamic_slice_in_dim(row_total, super_at * span_rows, span_rows, 1)
        ratio = jnp.exp(scores - top_rows[:, :, None]) / total_rows[:, :, None]
        return jnp.where(keep_mask, ratio, 0.0).astype(jnp.bfloat16)

    def output_step(step, carry):
        super_at, key_at, query_tile, key_tile, value_tile, keep_mask = tile_parts(step)

        def output_work(out_rows):
            scores = jnp.where(keep_mask, tile_scores(query_tile, key_tile, score_scale), NEG_FILL)
            weights = tile_weights(scores, super_at, keep_mask)
            value_heads = value_tile.reshape(BLK, HEADS, -1)
            part = jnp.einsum(
                "hqk,khd->qhd", weights, value_heads, preferred_element_type=jnp.float32
            ).reshape(span_rows, -1)
            current = lax.dynamic_slice_in_dim(out_rows, super_at * span_rows, span_rows, 0)
            return lax.dynamic_update_slice_in_dim(
                out_rows, current + part, super_at * span_rows, 0
            )

        return lax.cond(tile_any[super_at, key_at], output_work, unchanged, carry)

    partial_out = lax.fori_loop(0, tile_count, output_step, jnp.zeros((q_rows, D), jnp.float32))
    out_share = lax.psum_scatter(partial_out, "col", scatter_dimension=1, tiled=True).astype(
        jnp.bfloat16
    )
    grad_full, out_full = (
        lax.all_gather(cotangent, "col", axis=1, tiled=True),
        lax.all_gather(out_share, "col", axis=1, tiled=True),
    )
    delta = jnp.einsum(
        "qhd,qhd->hq",
        grad_full.reshape(q_rows, HEADS, -1),
        out_full.reshape(q_rows, HEADS, -1),
        preferred_element_type=jnp.float32,
    )

    def grad_step(step, carry):
        super_at, key_at, query_tile, key_tile, value_tile, keep_mask = tile_parts(step)

        def grad_work(state):
            query_accum, key_accum, value_accum = state
            scores = jnp.where(keep_mask, tile_scores(query_tile, key_tile, score_scale), NEG_FILL)
            weights = tile_weights(scores, super_at, keep_mask)
            grad_tile = lax.dynamic_slice_in_dim(
                grad_full, super_at * span_rows, span_rows, 0
            ).reshape(span_rows, HEADS, -1)
            value_heads = value_tile.reshape(BLK, HEADS, -1)
            key_heads = key_tile.reshape(BLK, HEADS, -1)
            query_heads = query_tile.reshape(span_rows, HEADS, -1)
            dweights = jnp.einsum(
                "qhd,khd->hqk", grad_tile, value_heads, preferred_element_type=jnp.float32
            )
            delta_rows = lax.dynamic_slice_in_dim(delta, super_at * span_rows, span_rows, 1)
            dscores = (weights.astype(jnp.float32) * (dweights - delta_rows[:, :, None])).astype(
                jnp.bfloat16
            )
            query_part = score_scale * jnp.einsum(
                "hqk,khd->qhd", dscores, key_heads, preferred_element_type=jnp.float32
            )
            key_part = score_scale * jnp.einsum(
                "hqk,qhd->khd", dscores, query_heads, preferred_element_type=jnp.float32
            )
            value_part = jnp.einsum(
                "hqk,qhd->khd", weights, grad_tile, preferred_element_type=jnp.float32
            )
            query_now = lax.dynamic_slice_in_dim(query_accum, super_at * span_rows, span_rows, 0)
            key_now = lax.dynamic_slice_in_dim(key_accum, key_at * BLK, BLK, 0)
            value_now = lax.dynamic_slice_in_dim(value_accum, key_at * BLK, BLK, 0)
            query_accum = lax.dynamic_update_slice_in_dim(
                query_accum, query_now + query_part.reshape(span_rows, -1), super_at * span_rows, 0
            )
            key_accum = lax.dynamic_update_slice_in_dim(
                key_accum, key_now + key_part.reshape(BLK, -1), key_at * BLK, 0
            )
            value_accum = lax.dynamic_update_slice_in_dim(
                value_accum, value_now + value_part.reshape(BLK, -1), key_at * BLK, 0
            )
            return (query_accum, key_accum, value_accum)

        return lax.cond(tile_any[super_at, key_at], grad_work, unchanged, carry)

    start_grads = (
        jnp.zeros((q_rows, D), jnp.float32),
        jnp.zeros((k_rows, D), jnp.float32),
        jnp.zeros((k_rows, D), jnp.float32),
    )
    query_parts, key_parts, value_parts = lax.fori_loop(0, tile_count, grad_step, start_grads)
    grad_queries = lax.psum_scatter(query_parts, "col", scatter_dimension=1, tiled=True).astype(
        jnp.bfloat16
    )
    grad_keys, grad_values = (
        lax.psum_scatter(key_parts, "row", scatter_dimension=1, tiled=True),
        lax.psum_scatter(value_parts, "row", scatter_dimension=1, tiled=True),
    )
    return (
        out_share,
        grad_queries,
        grad_keys.astype(jnp.bfloat16),
        grad_values.astype(jnp.bfloat16),
    )


def solution(mesh):
    rows, cols = mesh.shape["row"], mesh.shape["col"]
    one_head = rows == 4 and cols == 4
    return jax.shard_map(
        head_per_device if one_head else on_device,
        mesh=mesh,
        in_specs=(
            P(("groups", "row"), "col"),
            P(("groups", "col"), "row"),
            P(("groups", "col"), "row"),
            P(("groups", "row"), "col"),
            P(("groups", "row"), None),
            P(("groups", "row")),
        ),
        out_specs=(
            P(("groups", "row"), "col"),
            P(("groups", "row"), "col"),
            P(("groups", "col"), "row"),
            P(("groups", "col"), "row"),
        ),
        check_vma=False,
    )
```

```python
import functools
import math

import jax
import jax.numpy as jnp
from jax import lax
from jax.experimental import pallas as pl
from jax.experimental.pallas import tpu as pltpu
from jax.sharding import PartitionSpec as P

D = 1024
HEADS = 16
HEAD = 64
BLK = 128
MAXNB = 16


NEG_FILL = -1e30
GROUP = 2
STREAMS = 8
OUTS = 2
TAIL = 16
BATCHES = (1, 2, 1)
HOPS = (2, 3)
VMEM_LIMIT = 40 * 1024 * 1024
VMEM = pl.BlockSpec(memory_space=pltpu.VMEM)
SMEM = pl.BlockSpec(memory_space=pltpu.SMEM)


def pack_body(lists, counts, q_ref, g_ref, k_ref, v_ref, *outs):
    chunks = q_ref.shape[1] // HEAD
    rows = q_ref.shape[0]

    def pack(left_ref, right_ref, out_refs, at):
        for step in range(chunks):
            head = (at + step) % chunks
            lanes = slice(head * HEAD, (head + 1) * HEAD)
            out_refs[step][:rows, :] = jnp.concatenate(
                [left_ref[:, lanes], right_ref[:, lanes]], axis=1
            )

    for at in range(chunks):

        @pl.when(lax.axis_index("col") == at)
        def _():
            pack(k_ref, v_ref, outs[chunks:], at)

        @pl.when(lax.axis_index("row") == at)
        def _():
            pack(q_ref, g_ref, outs[:chunks], at)

    row = lax.broadcasted_iota(jnp.int32, (TAIL, 2 * HEAD), 0)
    lane = lax.broadcasted_iota(jnp.int32, (TAIL, 2 * HEAD), 1)
    table = jnp.zeros((TAIL, 2 * HEAD), jnp.int32)
    for qb in range(rows // BLK):
        line = jnp.where(lane == MAXNB, counts[qb], 0)
        for at in range(MAXNB):
            line = jnp.where(lane == at, lists[qb, at], line)
        table = jnp.where(row == qb, line, table)
    table = table.astype(jnp.float32).astype(jnp.bfloat16)
    for out_ref in outs[:chunks]:
        out_ref[rows:, :] = table


def unpack_body(axis, *refs):
    left_ref, right_ref = refs[-2:]
    chunks = len(refs) - 2
    for at in range(chunks):

        @pl.when(lax.axis_index(axis) == at)
        def _():
            parts = [refs[(head - at) % chunks][...] for head in range(chunks)]
            left_ref[...] = jnp.concatenate([p[:, :HEAD] for p in parts], axis=1)
            right_ref[...] = jnp.concatenate([p[:, HEAD:] for p in parts], axis=1)


def fold(x, op):
    return op(x.reshape(x.shape[0] // 8, 8, x.shape[1]), axis=0)


def attend_body(chunks, parts, first, last, *refs):
    def take(count):
        nonlocal refs
        head, refs = refs[:count], refs[count:]
        return head

    x_refs = take(chunks)
    if first:
        kv_refs = take(parts)
    else:
        kv_all, kv_t, acc_in = take(3)
    og_refs = take(chunks)
    gkv_refs = take(parts) if last else ()
    acc_out = () if last else take(1)
    if first:
        kv_all, kv_t = take(2)
    wide, table, items, both, both_t, stat, tiles, tops, sem, table_sem = take(10)
    outs, stats = take(OUTS), take(STREAMS)
    acc = take(1)[0] if last else acc_out[0]
    scale = 1.0 / math.sqrt(HEAD)
    to_log2 = scale * math.log2(math.e)
    rows = kv_all.shape[0] // parts
    per_chunk = rows // BLK
    blocks = chunks * per_chunk

    lane = lax.broadcasted_iota(jnp.int32, (TAIL, 2 * HEAD), 1)
    for c in range(chunks):
        listed = x_refs[c][rows:, :].astype(jnp.float32).astype(jnp.int32)
        part = lax.rem(lax.axis_index("col") - lax.div(listed, per_chunk) + parts, parts)
        slot = part * per_chunk + lax.rem(listed, per_chunk)
        wide[c * TAIL : (c + 1) * TAIL, :] = jnp.where(lane < MAXNB, slot, listed)
    table_copy = pltpu.make_async_copy(wide, table, table_sem)
    table_copy.start()

    copies = []
    if first:
        for c in range(parts):
            copies.append(
                pltpu.make_async_copy(
                    kv_refs[c], kv_all.at[pl.ds(c * rows, rows), :], sem.at[c]
                )
            )
    for copy in copies:
        copy.start()
    if first:
        acc[...] = jnp.zeros_like(acc)
    else:
        acc[...] = acc_in[...]
    for s in range(OUTS):
        outs[s][...] = jnp.zeros_like(outs[s])
    for s in range(STREAMS):
        stats[s][0] = jnp.full(stats[s].shape[1:], NEG_FILL, jnp.float32)
        stats[s][1] = jnp.zeros(stats[s].shape[1:], jnp.float32)
        stats[s][2] = jnp.zeros(stats[s].shape[1:], jnp.float32)

    is_left = lax.broadcasted_iota(jnp.int32, (BLK, 2 * HEAD), 1) < HEAD
    zeros = jnp.zeros((HEAD, BLK), jnp.bfloat16)
    for b in range(blocks):
        at = (b % per_chunk) * BLK
        x = x_refs[b // per_chunk][at : at + BLK, :]
        both[b, :BLK, :] = jnp.where(is_left, x, jnp.zeros_like(x))
        both[b, BLK:, :] = jnp.where(is_left, jnp.zeros_like(x), x)
        x_t = x.T
        both_t[b, :HEAD, :BLK] = x_t[:HEAD]
        both_t[b, :HEAD, BLK:] = zeros
        both_t[b, HEAD:, :BLK] = zeros
        both_t[b, HEAD:, BLK:] = x_t[HEAD:]
    if first:
        for c in range(parts):
            for b in range(per_chunk):
                at = c * rows + b * BLK
                kv_t[:, at : at + BLK] = kv_refs[c][b * BLK : (b + 1) * BLK, :].T
    for copy in copies:
        copy.wait()
    table_copy.wait()

    def line(qb):
        return lax.div(qb, per_chunk) * TAIL + lax.rem(qb, per_chunk)

    def add_items(qb, count):
        groups = (table[line(qb), MAXNB] + GROUP - 1) // GROUP

        def add_item(g, _):
            items[0, count + g] = qb
            items[1, count + g] = g * GROUP
            return 0

        lax.fori_loop(0, groups, add_item, 0)
        return count + groups

    count = lax.fori_loop(0, blocks, add_items, 0)
    steps = (count + STREAMS - 1) // STREAMS
    for s in range(STREAMS - 1):
        items[0, count + s] = 0
        items[1, count + s] = MAXNB

    def item(at):
        qb, base = items[0, at], items[1, at]
        slots = [
            pl.multiple_of(table[line(qb), jnp.minimum(base + u, MAXNB - 1)] * BLK, BLK)
            for u in range(GROUP)
        ]
        return qb, base, slots

    def score_step(i, _):
        for s in range(STREAMS):
            at = s * steps + i
            qb, base, slots = item(at)
            live = table[line(qb), MAXNB]
            kv = jnp.concatenate([kv_all[pl.ds(k, BLK), :] for k in slots], axis=0)
            both_scores = jnp.dot(kv, both_t[qb], preferred_element_type=jnp.float32)
            scores = [
                both_scores[u * BLK : (u + 1) * BLK, :BLK] * to_log2
                + jnp.where(base + u < live, 0.0, NEG_FILL)
                for u in range(GROUP)
            ]
            top = functools.reduce(jnp.maximum, [fold(v, jnp.max) for v in scores])
            top = jnp.max(top, axis=0, keepdims=True)
            total = jnp.zeros((8, BLK), jnp.float32)
            dot = jnp.zeros((8, BLK), jnp.float32)
            for u in range(GROUP):
                part = slice(u * BLK, (u + 1) * BLK)
                e = jnp.exp2(scores[u] - top)
                dw = both_scores[part, BLK:]
                tiles[at, part, :BLK] = e
                tiles[at, part, BLK:] = dw
                total = total + fold(e, jnp.sum)
                dot = dot + fold(e * dw, jnp.sum)
            total = jnp.sum(total, axis=0, keepdims=True)
            dot = jnp.sum(dot, axis=0, keepdims=True)
            tops[pl.ds(at, 1), :] = top
            row = pl.ds(qb, 1)
            old = stats[s][0, row, :]
            new = jnp.maximum(old, top)
            old_part, new_part = jnp.exp2(old - new), jnp.exp2(top - new)
            stats[s][0, row, :] = new
            stats[s][1, row, :] = stats[s][1, row, :] * old_part + total * new_part
            stats[s][2, row, :] = stats[s][2, row, :] * old_part + dot * new_part
        return 0

    lax.fori_loop(0, steps, score_step, 0)

    top = functools.reduce(jnp.maximum, [st[0] for st in stats])
    total = functools.reduce(jnp.add, [st[1] * jnp.exp2(st[0] - top) for st in stats])
    dot = functools.reduce(jnp.add, [st[2] * jnp.exp2(st[0] - top) for st in stats])
    stat[0] = top
    stat[1] = 1.0 / total
    stat[2] = dot / total

    def grad_step(i, _):
        for s in range(STREAMS):
            at = s * steps + i
            qb, base, slots = item(at)
            row = pl.ds(qb, 1)
            factor = stat[1, row, :] * jnp.exp2(tops[pl.ds(at, 1), :] - stat[0, row, :])
            delta = stat[2, row, :]
            w, ds = [], []
            for u in range(GROUP):
                part = slice(u * BLK, (u + 1) * BLK)
                weights = tiles[at, part, :BLK] * factor
                ds.append((weights * (tiles[at, part, BLK:] - delta)).astype(jnp.bfloat16))
                w.append(weights.astype(jnp.bfloat16))
            pair = jnp.concatenate(
                [jnp.concatenate(ds, axis=0), jnp.concatenate(w, axis=0)], axis=1
            )
            grads = jnp.dot(pair, both[qb], preferred_element_type=jnp.float32)
            for u in range(GROUP):
                acc[pl.ds(slots[u], BLK), :] += grads[u * BLK : (u + 1) * BLK]
            t = jnp.concatenate([kv_t[:, pl.ds(k, BLK)] for k in slots], axis=1)
            sums = jnp.dot(t, pair, preferred_element_type=jnp.float32)
            outs[s % OUTS][qb, :HEAD, :] += sums[HEAD:, BLK:]
            outs[s % OUTS][qb, HEAD:, :] += sums[:HEAD, :BLK]
        return 0

    lax.fori_loop(0, steps, grad_step, 0)

    is_out = lax.broadcasted_iota(jnp.int32, (2 * HEAD, BLK), 0) < HEAD
    for b in range(blocks):
        out = functools.reduce(jnp.add, [r[b] for r in outs])
        out = jnp.where(is_out, out, out * scale)
        at = (b % per_chunk) * BLK
        og_refs[b // per_chunk][at : at + BLK, :] = out.T.astype(jnp.bfloat16)
    if last:
        for b in range(parts * per_chunk):
            total = acc[b * BLK : (b + 1) * BLK, :]
            at = (b % per_chunk) * BLK
            gkv_refs[b // per_chunk][at : at + BLK, :] = jnp.where(
                is_left, total * scale, total
            ).astype(jnp.bfloat16)


def in_vmem(x):
    return pltpu.with_memory_space_constraint(x, pltpu.VMEM)


def head_per_device(queries, keys, values, cotangent, block_lists, block_counts):
    chunks = 4
    rows = queries.shape[0]
    chunk = pltpu.VMEM((rows, 2 * HEAD), jnp.bfloat16)
    tailed = pltpu.VMEM((rows + TAIL, 2 * HEAD), jnp.bfloat16)
    packed = pl.pallas_call(
        pack_body,
        out_shape=[tailed] * chunks + [chunk] * chunks,
        in_specs=[SMEM] * 2 + [VMEM] * 4,
        out_specs=[VMEM] * (2 * chunks),
        name="pack",
    )(block_lists, block_counts, queries, cotangent, keys, values)

    def q_perm(step):
        return [
            (r * chunks + c, c * chunks + (r + step) % chunks)
            for r in range(chunks)
            for c in range(chunks)
        ]

    def k_perm(step):
        return [(c, (c + step) % chunks) for c in range(chunks)]

    def swap(perm):
        return [(b, a) for a, b in perm]

    axes = ("row", "col")
    kv = [packed[chunks]] + [
        lax.ppermute(packed[chunks + s], "col", k_perm(s)) for s in range(1, chunks)
    ]
    hop = {s: lax.ppermute(packed[s], "col", [(c, c ^ 2) for c in range(chunks)]) for s in HOPS}
    xs = [
        lax.ppermute(
            hop.get(s, packed[s]), axes, [(a ^ 2, b) if s in hop else (a, b) for a, b in q_perm(s)]
        )
        for s in range(chunks)
    ]

    def attend(xs, carried, first, last):
        count = len(xs)
        blocks = count * rows // BLK
        most = blocks * MAXNB // GROUP + STREAMS
        keys_all = pltpu.VMEM((chunks * rows, 2 * HEAD), jnp.bfloat16)
        keys_t = pltpu.VMEM((2 * HEAD, chunks * rows), jnp.bfloat16)
        sums = pltpu.VMEM((chunks * rows, 2 * HEAD), jnp.float32)
        out_shape = [chunk] * count + ([chunk] * chunks if last else [sums])
        if first:
            out_shape += [keys_all, keys_t]
        return pl.pallas_call(
            functools.partial(attend_body, count, chunks, first, last),
            out_shape=out_shape,
            in_specs=[VMEM] * (count + len(carried)),
            out_specs=[VMEM] * len(out_shape),
            scratch_shapes=[
                pltpu.VMEM((count * TAIL, 2 * HEAD), jnp.int32),
                pltpu.SMEM((count * TAIL, 2 * HEAD), jnp.int32),
                pltpu.SMEM((2, most), jnp.int32),
                pltpu.VMEM((blocks, 2 * BLK, 2 * HEAD), jnp.bfloat16),
                pltpu.VMEM((blocks, 2 * HEAD, 2 * BLK), jnp.bfloat16),
                pltpu.VMEM((3, blocks, BLK), jnp.float32),
                pltpu.VMEM((most, GROUP * BLK, 2 * BLK), jnp.float32),
                pltpu.VMEM((most, BLK), jnp.float32),
                pltpu.SemaphoreType.DMA((chunks,)),
                pltpu.SemaphoreType.DMA,
            ]
            + [pltpu.VMEM((blocks, 2 * HEAD, BLK), jnp.float32)] * OUTS
            + [pltpu.VMEM((3, blocks, BLK), jnp.float32)] * STREAMS
            + ([sums] if last else []),
            compiler_params=pltpu.CompilerParams(vmem_limit_bytes=VMEM_LIMIT),
            name="attend",
        )(*[in_vmem(a) for a in (*xs, *carried)])

    carried = kv
    ogs = []
    for size in BATCHES:
        batch = xs[len(ogs) : len(ogs) + size]
        first, last = not ogs, len(ogs) + size == chunks
        results = attend(batch, carried, first, last)
        ogs += [
            lax.ppermute(results[s], axes, swap(q_perm(len(ogs) + s))) for s in range(size)
        ]
        rest = results[size:]
        if last:
            gkv = rest[:chunks]
        elif first:
            keys_all, keys_t = rest[1:]
        carried = [keys_all, keys_t, rest[0]] if not last else None
    gkv = [gkv[0]] + [lax.ppermute(gkv[s], "col", swap(k_perm(s))) for s in range(1, chunks)]

    whole = jax.ShapeDtypeStruct(queries.shape, jnp.bfloat16)

    def unpack(axis, parts):
        return pl.pallas_call(
            functools.partial(unpack_body, axis),
            out_shape=[whole, whole],
            in_specs=[VMEM] * chunks,
            out_specs=[VMEM, VMEM],
            name="unpack",
        )(*[in_vmem(p) for p in parts])

    attended, grad_queries = unpack("row", ogs)
    grad_keys, grad_values = unpack("col", gkv)
    return attended, grad_queries, grad_keys, grad_values


def tile_scores(query_tile, key_tile, score_scale):
    query_heads = query_tile.reshape(query_tile.shape[0], HEADS, -1)
    key_heads = key_tile.reshape(key_tile.shape[0], HEADS, -1)
    return (
        jnp.einsum("qhd,khd->hqk", query_heads, key_heads, preferred_element_type=jnp.float32)
        * score_scale
    )


def on_device(queries, keys, values, cotangent, block_lists, block_counts):
    score_scale = 1.0 / math.sqrt(HEAD)
    q_full = lax.all_gather(queries, "col", axis=1, tiled=True)
    k_full, v_full = (
        lax.all_gather(keys, "row", axis=1, tiled=True),
        lax.all_gather(values, "row", axis=1, tiled=True),
    )
    q_rows = q_full.shape[0]
    k_rows = k_full.shape[0]
    q_blocks = q_rows // BLK
    k_blocks = k_rows // BLK
    group_size = min(4, q_blocks)
    span_rows = group_size * BLK
    supers = q_blocks // group_size
    tile_count = supers * k_blocks
    first_key = lax.axis_index("col") * k_blocks
    wanted = first_key + jnp.arange(k_blocks, dtype=jnp.int32)
    live_slots = jnp.arange(MAXNB, dtype=jnp.int32)[None, :] < block_counts[:, None]
    block_hit = jnp.any(
        (block_lists[:, :, None] == wanted[None, None, :]) & live_slots[:, :, None], axis=1
    )
    block_hit = block_hit.reshape(supers, group_size, k_blocks).transpose(0, 2, 1)
    row_mask = jnp.repeat(block_hit, BLK, axis=2)
    tile_any = jnp.any(block_hit, axis=2)

    def tile_parts(step):
        super_at = step // k_blocks
        key_at = step % k_blocks
        query_tile = lax.dynamic_slice_in_dim(q_full, super_at * span_rows, span_rows, 0)
        key_tile = lax.dynamic_slice_in_dim(k_full, key_at * BLK, BLK, 0)
        value_tile = lax.dynamic_slice_in_dim(v_full, key_at * BLK, BLK, 0)
        keep_mask = row_mask[super_at, key_at][None, :, None]
        return (super_at, key_at, query_tile, key_tile, value_tile, keep_mask)

    def unchanged(carry):
        return carry

    def stats_step(step, carry):
        super_at, key_at, query_tile, key_tile, value_tile, keep_mask = tile_parts(step)

        def stats_work(state):
            row_top, row_total = state
            scores = jnp.where(keep_mask, tile_scores(query_tile, key_tile, score_scale), NEG_FILL)
            old_top = lax.dynamic_slice_in_dim(row_top, super_at * span_rows, span_rows, 1)
            old_total = lax.dynamic_slice_in_dim(row_total, super_at * span_rows, span_rows, 1)
            new_top = jnp.maximum(old_top, jnp.max(scores, axis=2))
            exp_terms = jnp.where(keep_mask, jnp.exp(scores - new_top[:, :, None]), 0.0)
            fresh = old_total * jnp.exp(old_top - new_top) + jnp.sum(exp_terms, axis=2)
            return (
                lax.dynamic_update_slice_in_dim(row_top, new_top, super_at * span_rows, 1),
                lax.dynamic_update_slice_in_dim(row_total, fresh, super_at * span_rows, 1),
            )

        return lax.cond(tile_any[super_at, key_at], stats_work, unchanged, carry)

    start_top = jnp.full((HEADS, q_rows), NEG_FILL, jnp.float32)
    start_total = jnp.zeros((HEADS, q_rows), jnp.float32)
    local_top, local_total = lax.fori_loop(0, tile_count, stats_step, (start_top, start_total))
    row_top = lax.pmax(local_top.astype(jnp.bfloat16), "col").astype(local_top.dtype)
    row_total = lax.psum(local_total * jnp.exp(local_top - row_top), "col")

    def tile_weights(scores, super_at, keep_mask):
        top_rows = lax.dynamic_slice_in_dim(row_top, super_at * span_rows, span_rows, 1)
        total_rows = lax.dynamic_slice_in_dim(row_total, super_at * span_rows, span_rows, 1)
        ratio = jnp.exp(scores - top_rows[:, :, None]) / total_rows[:, :, None]
        return jnp.where(keep_mask, ratio, 0.0).astype(jnp.bfloat16)

    def output_step(step, carry):
        super_at, key_at, query_tile, key_tile, value_tile, keep_mask = tile_parts(step)

        def output_work(out_rows):
            scores = jnp.where(keep_mask, tile_scores(query_tile, key_tile, score_scale), NEG_FILL)
            weights = tile_weights(scores, super_at, keep_mask)
            value_heads = value_tile.reshape(BLK, HEADS, -1)
            part = jnp.einsum(
                "hqk,khd->qhd", weights, value_heads, preferred_element_type=jnp.float32
            ).reshape(span_rows, -1)
            current = lax.dynamic_slice_in_dim(out_rows, super_at * span_rows, span_rows, 0)
            return lax.dynamic_update_slice_in_dim(
                out_rows, current + part, super_at * span_rows, 0
            )

        return lax.cond(tile_any[super_at, key_at], output_work, unchanged, carry)

    partial_out = lax.fori_loop(0, tile_count, output_step, jnp.zeros((q_rows, D), jnp.float32))
    out_share = lax.psum_scatter(partial_out, "col", scatter_dimension=1, tiled=True).astype(
        jnp.bfloat16
    )
    grad_full, out_full = (
        lax.all_gather(cotangent, "col", axis=1, tiled=True),
        lax.all_gather(out_share, "col", axis=1, tiled=True),
    )
    delta = jnp.einsum(
        "qhd,qhd->hq",
        grad_full.reshape(q_rows, HEADS, -1),
        out_full.reshape(q_rows, HEADS, -1),
        preferred_element_type=jnp.float32,
    )

    def grad_step(step, carry):
        super_at, key_at, query_tile, key_tile, value_tile, keep_mask = tile_parts(step)

        def grad_work(state):
            query_accum, key_accum, value_accum = state
            scores = jnp.where(keep_mask, tile_scores(query_tile, key_tile, score_scale), NEG_FILL)
            weights = tile_weights(scores, super_at, keep_mask)
            grad_tile = lax.dynamic_slice_in_dim(
                grad_full, super_at * span_rows, span_rows, 0
            ).reshape(span_rows, HEADS, -1)
            value_heads = value_tile.reshape(BLK, HEADS, -1)
            key_heads = key_tile.reshape(BLK, HEADS, -1)
            query_heads = query_tile.reshape(span_rows, HEADS, -1)
            dweights = jnp.einsum(
                "qhd,khd->hqk", grad_tile, value_heads, preferred_element_type=jnp.float32
            )
            delta_rows = lax.dynamic_slice_in_dim(delta, super_at * span_rows, span_rows, 1)
            dscores = (weights.astype(jnp.float32) * (dweights - delta_rows[:, :, None])).astype(
                jnp.bfloat16
            )
            query_part = score_scale * jnp.einsum(
                "hqk,khd->qhd", dscores, key_heads, preferred_element_type=jnp.float32
            )
            key_part = score_scale * jnp.einsum(
                "hqk,qhd->khd", dscores, query_heads, preferred_element_type=jnp.float32
            )
            value_part = jnp.einsum(
                "hqk,qhd->khd", weights, grad_tile, preferred_element_type=jnp.float32
            )
            query_now = lax.dynamic_slice_in_dim(query_accum, super_at * span_rows, span_rows, 0)
            key_now = lax.dynamic_slice_in_dim(key_accum, key_at * BLK, BLK, 0)
            value_now = lax.dynamic_slice_in_dim(value_accum, key_at * BLK, BLK, 0)
            query_accum = lax.dynamic_update_slice_in_dim(
                query_accum, query_now + query_part.reshape(span_rows, -1), super_at * span_rows, 0
            )
            key_accum = lax.dynamic_update_slice_in_dim(
                key_accum, key_now + key_part.reshape(BLK, -1), key_at * BLK, 0
            )
            value_accum = lax.dynamic_update_slice_in_dim(
                value_accum, value_now + value_part.reshape(BLK, -1), key_at * BLK, 0
            )
            return (query_accum, key_accum, value_accum)

        return lax.cond(tile_any[super_at, key_at], grad_work, unchanged, carry)

    start_grads = (
        jnp.zeros((q_rows, D), jnp.float32),
        jnp.zeros((k_rows, D), jnp.float32),
        jnp.zeros((k_rows, D), jnp.float32),
    )
    query_parts, key_parts, value_parts = lax.fori_loop(0, tile_count, grad_step, start_grads)
    grad_queries = lax.psum_scatter(query_parts, "col", scatter_dimension=1, tiled=True).astype(
        jnp.bfloat16
    )
    grad_keys, grad_values = (
        lax.psum_scatter(key_parts, "row", scatter_dimension=1, tiled=True),
        lax.psum_scatter(value_parts, "row", scatter_dimension=1, tiled=True),
    )
    return (
        out_share,
        grad_queries,
        grad_keys.astype(jnp.bfloat16),
        grad_values.astype(jnp.bfloat16),
    )


def solution(mesh):
    rows, cols = mesh.shape["row"], mesh.shape["col"]
    one_head = rows == 4 and cols == 4
    return jax.shard_map(
        head_per_device if one_head else on_device,
        mesh=mesh,
        in_specs=(
            P(("groups", "row"), "col"),
            P(("groups", "col"), "row"),
            P(("groups", "col"), "row"),
            P(("groups", "row"), "col"),
            P(("groups", "row"), None),
            P(("groups", "row")),
        ),
        out_specs=(
            P(("groups", "row"), "col"),
            P(("groups", "row"), "col"),
            P(("groups", "col"), "row"),
            P(("groups", "col"), "row"),
        ),
        check_vma=False,
    )
```
